32 devices in a mesh: groups: 2 (over x), ctx: 8 (over z, y), head: 2 (over core).
Axes of the slice: x: 2, y: 2, z: 4, core: 2. Of those that a mesh axis runs over, the one named last changes fastest.
Arguments:
- queries: bfloat16 [4096, 2048], P(('groups', 'ctx'), 'head'), parts along dimension 0, may hold values from -12 to 12
- span_keys: bfloat16 [4096, 2048], P(('groups', 'ctx'), 'head'), parts along dimension 0, may hold values from -12 to 12
- span_values: bfloat16 [4096, 2048], P(('groups', 'ctx'), 'head'), parts along dimension 0, may hold values from -6 to 6
- cache_keys: bfloat16 [8192, 2048], P(('groups', 'ctx'), 'head'), parts along dimension 0, may hold values from -12 to 12
- cache_values: bfloat16 [8192, 2048], P(('groups', 'ctx'), 'head'), parts along dimension 0, may hold values from -6 to 6
- routes: int32 [2, 32, 8, 4], P('head', ('groups', 'ctx')), parts along dimension 1, may hold values from 0 to 7, all different within a row; in each aligned block of 16 rows (0 to 15, 16 to 31, ..., all dimensions but the last counted through in order) at most 16 rows name the same one
- out_weight: bfloat16 [2048, 4096], P('head'), may hold values from -0.125 to 0.125
Outputs:
- projected: bfloat16 [4096, 4096], P(('groups', 'ctx'), 'head'), parts along dimension 0
The draws below stay inside these ranges and needn't reach their ends.
There are 2 independent parts, one for each index of `groups`. The reference program is written for one: setup_inputs(seed, part) draws one part's arguments, and reference() takes and returns one part's arrays. A program takes and returns all parts, laid end to end along the dimension named above; an argument that names none is the same for every part. Nothing has to cross between parts.
Inputs may be any that keep to these rules, and one draw needn't show every extreme that they name: `routes`: each row names 4 different key blocks; among the 16 rows of one device no key block is named more than 16 times.
All inputs are finite; a program needn't handle non-finite values.
Results may differ from the reference program's by a relative error of at most 0.0064.
Values may be sent and summed in bfloat16 or wider, within the bound.
A program may use at most 128 MiB of HBM per device.

```python
import math
import jax
import jax.numpy as jnp
import numpy as np
from jax import lax

D = 4096
HEADS = 16
DH = 128
QB = 128
KB = 512
TOP = 4
QBLK_DEV = 2
HEADS_DEV = 8
NQB = 16
QTOK = 2048
NKB = 8
CTXLEN = 4096
MOST = 16
N_HEAD = 2


def keys_like(key, salt, row_count):
    shape = (row_count, HEADS, DH)
    noise = jnp.clip(jax.random.normal(jax.random.fold_in(key, salt), shape, jnp.float32), -6.0, 6.0)
    return noise.reshape(row_count, HEADS * DH).astype(jnp.bfloat16)


def draw_queries(key, part):
    shape = (QTOK, HEADS, DH)
    noise = jnp.clip(jax.random.normal(jax.random.fold_in(key, 1), shape, jnp.float32), -6.0, 6.0)
    return noise.reshape(QTOK, HEADS * DH).astype(jnp.bfloat16)


def draw_span_keys(key, part):
    return keys_like(key, 3, QTOK)


def draw_cache_keys(key, part):
    return keys_like(key, 4, CTXLEN)


def steps_of(rng, shape, split, smallest, top_value):
    level, own = 1.0, jax.random.fold_in(rng, 6)
    for dim, shards_of in split:
        draws = jnp.exp(jax.random.uniform(jax.random.fold_in(own, dim), (shards_of,), jnp.float32, smallest / len(split), top_value / len(split)))
        level = level * jnp.repeat(draws, shape[dim] // shards_of).reshape([-1 if axis == dim else 1 for axis in range(len(shape))])
    return level


def shared_out(stream_key, own, number, rows, amount, top, limit, slope):
    order = jax.random.permutation(stream_key, amount)
    crowded, usual = shares(amount, rows * top, limit, slope, True), shares(amount, rows * top, limit, slope, False)
    places = jnp.arange(amount)

    def named(lengths, offset_by):
        used = int((lengths > 0).sum())
        fixed = max(1, used // 4)
        shifted = fixed + (places - fixed + offset_by * (used - fixed)) % max(1, amount - fixed)
        return jnp.zeros((amount,), jnp.int32).at[order[jnp.where(places < fixed, places, shifted)]].set(jnp.asarray(lengths, jnp.int32))

    lengths = jnp.where(number % 4 == 0, named(crowded, number // 4), named(usual, number - number // 4 - 1))
    mixed = jax.random.permutation(jax.random.fold_in(own, 3), amount)
    giver, receiver = mixed[0:amount // 2 * 2:2], mixed[1:amount // 2 * 2:2]
    margin = jnp.minimum(lengths[giver] - 1, limit - lengths[receiver]) // 2
    margin = jnp.where((giver == order[0]) | (receiver == order[0]) | (lengths[receiver] == 0), 0, jnp.maximum(margin, 0))
    shifted = jax.random.randint(jax.random.fold_in(own, 4), (amount // 2,), 0, 1 << 20) % (margin + 1)
    lengths = lengths.at[giver].add(-shifted).at[receiver].add(shifted)
    labels = jnp.searchsorted(jnp.cumsum(lengths), jnp.arange(rows * top), side="right").astype(jnp.int32)
    grid = labels.reshape(top, rows).T
    grid = grid[jax.random.permutation(jax.random.fold_in(own, 1), rows)]
    offset_by = jax.random.randint(jax.random.fold_in(own, 2), (rows, 1), 0, top)
    return jnp.take_along_axis(grid, (jnp.arange(top)[None, :] + offset_by) % top, axis=1)


def shares(amount, total, most, slope, full):
    portions = [(1 << 20) // math.isqrt(grade ** slope) + 1 for grade in range(1, amount + 1)]
    largest = most if full else min(most, max(-(-total // amount), total * portions[0] // sum(portions)))
    least = 1 if total - largest >= amount - 1 else 0
    counts, spare = [largest] + [least] * (amount - 1), total - largest - least * (amount - 1)
    while spare > 0:
        movable = [i for i in range(1, amount) if counts[i] < largest] or [i for i in range(1, amount) if counts[i] < most]
        mass, remaining = sum([portions[i] for i in movable]), spare
        for i in movable:
            extra = min(most - counts[i], max(1, remaining * portions[i] // mass), spare)
            counts[i] = counts[i] + extra
            spare = spare - extra
    return np.array(counts)


def gaussian(stream_key, dims, scale, limit, pieces=(), held_as=jnp.bfloat16):
    values = scale * jax.random.normal(stream_key, dims, jnp.float32)
    if pieces:
        values = values * steps_of(stream_key, dims, pieces, -0.22, 0.18)
    return jnp.clip(values, -limit, limit).astype(held_as)


def setup_inputs(seed: int = 0, part: int = 0) -> dict:
    keys = jax.random.split(jax.random.key(seed), 8)
    part_keys = jax.random.split(jax.random.fold_in(keys[7], part), 8)
    queries = draw_queries(jax.random.fold_in(jax.random.fold_in(keys[7], part), 71), part)
    span_keys = draw_span_keys(jax.random.fold_in(jax.random.fold_in(keys[7], part), 71), part)
    span_values = gaussian(part_keys[2], (QTOK, HEADS * DH), 1.0, 6.0, ((0, 8), (1, 2)))
    cache_keys = draw_cache_keys(jax.random.fold_in(jax.random.fold_in(keys[7], part), 71), part)
    cache_values = gaussian(part_keys[4], (CTXLEN, HEADS * DH), 1.0, 6.0, ((0, 8), (1, 2)))
    routes_keys = jax.random.split(jax.random.fold_in(part_keys[5], 1), N_HEAD * NQB * HEADS_DEV // (QBLK_DEV * HEADS_DEV))
    routes_turns = jax.random.permutation(jax.random.fold_in(part_keys[5], 3), N_HEAD * NQB * HEADS_DEV // (QBLK_DEV * HEADS_DEV))
    routes = jax.vmap(lambda own, number: shared_out(jax.random.fold_in(part_keys[5], 2), own, number, QBLK_DEV * HEADS_DEV, NKB, TOP, MOST, 2))(routes_keys, routes_turns).reshape((N_HEAD, NQB, HEADS_DEV, TOP))
    out_weight = gaussian(keys[6], (HEADS * DH, D), (HEADS * DH) ** -0.5, 0.125, ((0, 2),))
    return dict(queries=queries, span_keys=span_keys, span_values=span_values, cache_keys=cache_keys, cache_values=cache_values, routes=routes, out_weight=out_weight)


def soft_partial(scores, values_block, pattern):
    highest = jnp.max(scores, axis=-1, keepdims=True)
    exponent = jnp.exp(scores - highest)
    denominator = jnp.sum(exponent, axis=-1, keepdims=True)
    weights_low = lax.optimization_barrier((exponent / denominator).astype(jnp.bfloat16))
    result = jnp.einsum(pattern, weights_low.astype(jnp.float32), values_block.astype(jnp.float32))
    result = lax.optimization_barrier(result.astype(jnp.bfloat16))
    log_total = highest[..., 0] + jnp.log(denominator[..., 0])
    return result, log_total


def reference(queries, span_keys, span_values, cache_keys, cache_values, routes, out_weight):
    scaling = DH ** -0.5
    blocked = queries.reshape(NQB, QB, HEADS, DH)
    own_keys = span_keys.reshape(NQB, QB, HEADS, DH)
    own_values = span_values.reshape(NQB, QB, HEADS, DH)
    keys_by_head = cache_keys.reshape(NKB, KB, HEADS, DH).transpose(2, 0, 1, 3)
    values_by_head = cache_values.reshape(NKB, KB, HEADS, DH).transpose(2, 0, 1, 3)
    route_table = routes.transpose(1, 0, 2, 3).reshape(NQB, HEADS, TOP).astype(jnp.int32)
    causal = jnp.arange(QB)[:, None] >= jnp.arange(QB)[None, :]
    head_ids = jnp.arange(HEADS, dtype=jnp.int32)[:, None]

    def one_block(packed):
        query_rows, self_keys, self_values, chosen = packed
        query_float = query_rows.astype(jnp.float32)
        picked_keys = keys_by_head[head_ids, chosen]
        picked_values = values_by_head[head_ids, chosen]
        routed_scores = jnp.einsum("qhd,htkd->htqk", query_float, picked_keys.astype(jnp.float32)) * scaling
        routed_out, routed_lse = soft_partial(routed_scores, picked_values, "htqk,htkd->htqd")
        self_scores = jnp.einsum("qhd,khd->hqk", query_float, self_keys.astype(jnp.float32)) * scaling
        self_scores = jnp.where(causal[None], self_scores, -jnp.inf)
        self_out, self_lse = soft_partial(self_scores, self_values, "hqk,khd->hqd")
        all_lse = jnp.concatenate([routed_lse, self_lse[:, None]], axis=1)
        all_out = jnp.concatenate([routed_out, self_out[:, None]], axis=1)
        highest = jnp.max(all_lse, axis=1, keepdims=True)
        merge_weights = jnp.exp(all_lse - highest)
        merge_weights = merge_weights / jnp.sum(merge_weights, axis=1, keepdims=True)
        attention = jnp.sum(merge_weights[..., None] * all_out.astype(jnp.float32), axis=1)
        return attention.transpose(1, 0, 2).reshape(QB, HEADS * DH).astype(jnp.bfloat16)

    attention = lax.map(one_block, (blocked, own_keys, own_values, route_table)).reshape(QTOK, HEADS * DH)
    return jnp.dot(attention, out_weight, preferred_element_type=jnp.float32).astype(jnp.bfloat16)
```

```python
import functools
import math

import jax
import jax.numpy as jnp
from jax import lax
from jax.experimental import pallas as pl
from jax.experimental.pallas import tpu as pltpu
from jax.sharding import PartitionSpec as P

DH = 128
QB = 128


def shortened(value):

    def short(part):
        return part.astype(jnp.bfloat16) if part.dtype == jnp.float32 else part

    return jax.tree.map(short, value)


def soft_partial(scores, values_block, pattern):
    highest = jnp.max(scores, axis=-1, keepdims=True)
    exponent = jnp.exp(scores - highest)
    denominator = jnp.sum(exponent, axis=-1, keepdims=True)
    weights_low = (exponent / denominator).astype(jnp.bfloat16)
    result = jnp.einsum(
        pattern, weights_low, values_block, preferred_element_type=jnp.float32
    ).astype(jnp.bfloat16)
    log_total = highest[..., 0] + jnp.log(denominator[..., 0])
    return (result, log_total)


def routed_by_slots(queries, span_keys, span_values, cache_keys, cache_values, routes, out_weight):
    blocks = routes.shape[1]
    heads_here = routes.shape[2]
    top_picks = routes.shape[3]
    key_rows = cache_keys.shape[0]
    devices = lax.axis_size("ctx")
    scaling = 1.0 / math.sqrt(DH)
    blocked = queries.reshape(blocks, QB, heads_here, DH)
    most_rows = max(2, 2 * blocks * heads_here * top_picks // devices)
    groups = 1
    per_peer = groups * most_rows
    slot_total = per_peer * devices
    wanted = routes.reshape(-1)
    item_count = wanted.shape[0]
    item_ids = jnp.arange(item_count, dtype=jnp.int32)
    block_of = item_ids // (heads_here * top_picks)
    head_of = item_ids // top_picks % heads_here
    bucket = wanted * groups + block_of % groups
    one_hot = (bucket[:, None] == jnp.arange(devices * groups, dtype=jnp.int32)[None, :]).astype(
        jnp.int32
    )
    ranking = jnp.sum(jnp.cumsum(one_hot, axis=0) * one_hot, axis=1) - 1
    position = (block_of % groups * most_rows + ranking) * devices + wanted
    matches = position[None, :] == jnp.arange(slot_total, dtype=jnp.int32)[:, None]
    filled = jnp.any(matches, axis=1)
    source = jnp.sum(jnp.where(matches, item_ids[None, :], 0), axis=1)
    gathered = blocked[block_of[source], :, head_of[source], :]
    slot_queries = jnp.where(filled[:, None, None], gathered, jnp.zeros_like(gathered)).reshape(
        per_peer, devices, QB, DH
    )
    slot_heads = jnp.where(filled, head_of[source], 0).reshape(per_peer, devices)
    keys_by_head = cache_keys.reshape(key_rows, heads_here, DH).transpose(1, 0, 2)
    values_by_head = cache_values.reshape(key_rows, heads_here, DH).transpose(1, 0, 2)

    def one_portion(portion):
        queried, head_ids = portion
        chosen_keys = keys_by_head[head_ids]
        chosen_values = values_by_head[head_ids]
        scores = (
            jnp.einsum("pqd,pkd->pqk", queried, chosen_keys, preferred_element_type=jnp.float32)
            * scaling
        )
        return soft_partial(scores, chosen_values, "pqk,pkd->pqd")

    outputs, log_sums = lax.map(
        one_portion,
        (
            lax.all_to_all(slot_queries, "ctx", split_axis=1, concat_axis=1, tiled=True),
            lax.all_to_all(slot_heads, "ctx", split_axis=1, concat_axis=1, tiled=True),
        ),
    )
    outputs_back = jax.tree.map(
        lambda part, own: part.astype(own.dtype),
        lax.all_to_all(shortened(outputs), "ctx", split_axis=1, concat_axis=1, tiled=True),
        outputs,
    )
    sums_back = lax.all_to_all(log_sums, "ctx", split_axis=1, concat_axis=1, tiled=True)
    routed_out = outputs_back.reshape(slot_total, QB, DH)[position].reshape(
        blocks, heads_here, top_picks, QB, DH
    )
    routed_lse = sums_back.reshape(slot_total, QB)[position].reshape(
        blocks, heads_here, top_picks, QB
    )
    own_keys = span_keys.reshape(blocks, QB, heads_here, DH)
    own_values = span_values.reshape(blocks, QB, heads_here, DH)
    causal = jnp.arange(QB)[:, None] >= jnp.arange(QB)[None, :]
    self_scores = (
        jnp.einsum("bqhd,bkhd->bhqk", blocked, own_keys, preferred_element_type=jnp.float32)
        * scaling
    )
    self_scores = jnp.where(causal[None, None], self_scores, -jnp.inf)
    self_out, self_lse = soft_partial(self_scores, own_values, "bhqk,bkhd->bhqd")
    all_lse = jnp.concatenate([routed_lse, self_lse[:, :, None]], axis=2)
    all_out = jnp.concatenate(
        [routed_out.astype(jnp.float32), self_out[:, :, None].astype(jnp.float32)], axis=2
    )
    highest = jnp.max(all_lse, axis=2, keepdims=True)
    merge_weights = jnp.exp(all_lse - highest)
    merge_weights = merge_weights / jnp.sum(merge_weights, axis=2, keepdims=True)
    attention = jnp.sum(merge_weights[..., None] * all_out, axis=2)
    attention = (
        attention.transpose(0, 2, 1, 3).reshape(blocks * QB, heads_here * DH).astype(jnp.bfloat16)
    )
    partial_sums = jnp.dot(attention, out_weight, preferred_element_type=jnp.float32)
    return lax.psum_scatter(partial_sums, "head", scatter_dimension=1, tiled=True).astype(
        jnp.bfloat16
    )


BIG = 1e30
LOG2E = math.log2(math.e)
EXTRA = 16


def packed_rows(out, lse):
    high = lse.astype(jnp.bfloat16)
    rest = lse - high.astype(jnp.float32)
    middle = rest.astype(jnp.bfloat16)
    low = (rest - middle.astype(jnp.float32)).astype(jnp.bfloat16)
    row = lax.broadcasted_iota(jnp.int32, (EXTRA, lse.shape[1]), 0)
    tail = jnp.where(
        row == 0,
        high.astype(jnp.float32),
        jnp.where(
            row == 1,
            middle.astype(jnp.float32),
            jnp.where(row == 2, low.astype(jnp.float32), 0.0),
        ),
    )
    return out.astype(jnp.bfloat16), tail.astype(jnp.bfloat16)


def store_message(ref, out, lse):
    body, tail = packed_rows(out, lse)
    ref[0:DH, :] = body
    ref[DH : DH + EXTRA, :] = tail


def load_message(ref):
    out = ref[0:DH, :].astype(jnp.float32)
    lse = jnp.sum(ref[DH : DH + EXTRA, :].astype(jnp.float32), axis=0, keepdims=True)
    return out, lse


def merged(first, second):
    out_a, lse_a = first
    out_b, lse_b = second
    top = jnp.maximum(lse_a, lse_b)
    weight_a = jnp.exp2(lse_a - top)
    weight_b = jnp.exp2(lse_b - top)
    total = weight_a + weight_b
    return (
        out_a * (weight_a / total) + out_b * (weight_b / total),
        top + jnp.log2(total),
    )


def kernel(
    stages,
    heads,
    blocks,
    q_ref,
    flag_ref,
    span_k,
    span_v,
    k_ref,
    v_ref,
    w_hbm,
    y_ref,
    qg,
    kr,
    vr,
    part,
    from_left,
    from_right,
    selfp,
    att,
    wv,
    ag_send,
    ag_recv,
    rs_send,
    rs_recv,
    kv_send,
    kv_recv,
    att_send,
    att_recv,
    w_sem,
):
    rows = blocks * QB
    span = k_ref.shape[0]
    width = heads * DH
    columns = y_ref.shape[1]
    me = lax.axis_index("ctx")
    core = lax.axis_index("head")
    z = me // 2
    y = me % 2
    pair = me + 1 - 2 * y
    other = 1 - core
    has_left = z > 0
    has_right = z < stages - 1
    scale = LOG2E / math.sqrt(DH)

    def head_columns(h):
        return pl.ds(pl.multiple_of(h * DH, DH), DH)

    barrier = pltpu.get_barrier_semaphore()
    pl.semaphore_signal(barrier, inc=1, device_id={"ctx": pair})
    pl.semaphore_signal(barrier, inc=1, device_id={"head": other})

    @pl.when(has_left)
    def _():
        pl.semaphore_signal(barrier, inc=1, device_id={"ctx": me - 2})

    @pl.when(has_right)
    def _():
        pl.semaphore_signal(barrier, inc=1, device_id={"ctx": me + 2})

    for h in range(heads):
        qg[z, h, 0:rows, :] = q_ref[:, h * DH : (h + 1) * DH]
        qg[z, h, rows:, :] = flag_ref[h]

    pl.semaphore_wait(
        barrier, 2 + jnp.minimum(z, 1) + jnp.minimum(stages - 1 - z, 1)
    )

    def kv_copies(h):
        return (
            pltpu.make_async_remote_copy(
                src_ref=k_ref.at[:, head_columns(h)],
                dst_ref=kr.at[h],
                send_sem=kv_send.at[0, h],
                recv_sem=kv_recv.at[0, h],
                device_id={"ctx": pair},
            ),
            pltpu.make_async_remote_copy(
                src_ref=v_ref.at[:, head_columns(h)],
                dst_ref=vr.at[h],
                send_sem=kv_send.at[1, h],
                recv_sem=kv_recv.at[1, h],
                device_id={"ctx": pair},
            ),
        )

    def ag_copy(h, source, step):
        return pltpu.make_async_remote_copy(
            src_ref=qg.at[source, h],
            dst_ref=qg.at[source, h],
            send_sem=ag_send.at[(step + 1) // 2, h, source],
            recv_sem=ag_recv.at[h, source],
            device_id={"ctx": me + 2 * step},
        )

    def rs_copy(h, dest, step):
        return pltpu.make_async_remote_copy(
            src_ref=part.at[h, dest],
            dst_ref=(from_left if step > 0 else from_right).at[h, dest],
            send_sem=rs_send.at[h, dest],
            recv_sem=rs_recv.at[(step + 1) // 2, h, dest],
            device_id={"ctx": me + 2 * step},
        )

    def att_copy(h):
        place = pl.ds(pl.multiple_of(core * width + h * DH, DH), DH)
        return pltpu.make_async_remote_copy(
            src_ref=att.at[:, place],
            dst_ref=att.at[:, place],
            send_sem=att_send.at[h],
            recv_sem=att_recv.at[h],
            device_id={"head": other},
        )

    w_rows = pl.ds(pl.multiple_of(core * width, DH), width)
    w_remote = pltpu.make_async_remote_copy(
        src_ref=w_hbm.at[:, pl.ds(pl.multiple_of(other * columns, DH), columns)],
        dst_ref=wv.at[w_rows, :],
        send_sem=w_sem.at[0],
        recv_sem=w_sem.at[1],
        device_id={"head": other},
    )
    w_local = pltpu.make_async_copy(
        w_hbm.at[:, pl.ds(pl.multiple_of(core * columns, DH), columns)],
        wv.at[w_rows, :],
        w_sem.at[2],
    )

    @pl.loop(0, heads)
    def _(h):
        for copy in kv_copies(h):
            copy.start()

    def gather_step(t):
        for a in range(stages):
            h = t - a

            @pl.when((h >= 0) & (h < heads))
            def _():
                for step in (1, -1):
                    source = z - a * step
                    here = (source >= 0) & (source < stages)
                    onward = has_right if step > 0 else has_left

                    @pl.when(here)
                    def _():
                        if a > 0:
                            ag_copy(h, source, step).wait_recv()

                        @pl.when(onward)
                        def _():
                            ag_copy(h, source, step).start()

    def compute(h):
        for copy in kv_copies(h):
            copy.wait_recv()
        keys = (k_ref.at[:, head_columns(h)], kr.at[h])
        values_t = (v_ref[:, head_columns(h)].T, vr[h].T)

        @pl.loop(0, stages)
        def _(s):
            queried = qg[s, h, 0:rows, :]
            flags = qg[s, h, rows:, :].astype(jnp.float32)
            row = lax.broadcasted_iota(jnp.int32, flags.shape, 0)
            routed, scores, highest = [], [], None
            for at, number in enumerate((me, pair)):
                chosen = jnp.concatenate(
                    [
                        jnp.sum(
                            jnp.where(row == number * blocks + j, flags, 0.0),
                            axis=0,
                            keepdims=True,
                        )
                        for j in range(blocks)
                    ],
                    axis=1,
                )
                score = lax.dot_general(
                    keys[at][...],
                    queried,
                    (((1,), (1,)), ((), ())),
                    preferred_element_type=jnp.float32,
                )
                top = jnp.where(
                    chosen > 0.0, jnp.max(score, axis=0, keepdims=True) * scale, -BIG
                )
                highest = top if highest is None else jnp.maximum(highest, top)
                routed.append(chosen)
                scores.append(score)
            total, out = None, None
            for at in range(2):
                shift = jnp.where(routed[at] > 0.0, highest, BIG)
                exponent = jnp.exp2(scores[at] * scale - shift)
                portion = jnp.sum(exponent, axis=0, keepdims=True)
                result = jnp.dot(
                    values_t[at],
                    exponent.astype(jnp.bfloat16),
                    preferred_element_type=jnp.float32,
                )
                total = portion if total is None else total + portion
                out = result if out is None else out + result
            safe = jnp.maximum(total, 0.5)
            store_message(
                part.at[h, s],
                out * (1.0 / safe),
                jnp.where(total > 0.0, highest + jnp.log2(safe), -BIG),
            )

    def self_part(h):
        for j in range(blocks):
            here = pl.ds(j * QB, QB)
            score = lax.dot_general(
                span_k[here, head_columns(h)],
                q_ref[here, head_columns(h)],
                (((1,), (1,)), ((), ())),
                preferred_element_type=jnp.float32,
            )
            shape = (QB, QB)
            causal = lax.broadcasted_iota(jnp.int32, shape, 0) <= lax.broadcasted_iota(
                jnp.int32, shape, 1
            )
            score = jnp.where(causal, score * scale, -BIG)
            top = jnp.max(score, axis=0, keepdims=True)
            exponent = jnp.exp2(score - top)
            total = jnp.sum(exponent, axis=0, keepdims=True)
            out = jnp.dot(
                span_v[here, head_columns(h)].T,
                exponent.astype(jnp.bfloat16),
                preferred_element_type=jnp.float32,
            )
            store_message(
                selfp.at[h, :, j * QB : (j + 1) * QB], out * (1.0 / total), top + jnp.log2(total)
            )

    def reduce_step(h, step):
        arrived = from_left if step > 0 else from_right
        first = ~has_left if step > 0 else ~has_right

        @pl.when((h >= 0) & (h < heads))
        def _():
            for dest in range(stages):
                ahead = (dest - z) * step

                @pl.when((ahead >= 0) & ~first)
                def _():
                    rs_copy(h, dest, step).wait_recv()
                    store_message(
                        part.at[h, dest],
                        *merged(
                            load_message(part.at[h, dest]), load_message(arrived.at[h, dest])
                        ),
                    )

                @pl.when(ahead > 0)
                def _():
                    rs_copy(h, dest, step).start()

    def finish(h):
        out, _ = merged(load_message(part.at[h, z]), load_message(selfp.at[h]))
        place = pl.ds(pl.multiple_of(core * width + h * DH, DH), DH)
        att[:, place] = out.T.astype(jnp.bfloat16)
        att_copy(h).start()

    gather_step(0)
    w_remote.start()
    w_local.start()

    @pl.loop(0, heads)
    def _(h):
        self_part(h)

    last = stages - 1

    @pl.loop(1, heads + 2 * last + 1)
    def _(t):
        gather_step(t)

        @pl.when((t >= last) & (t < heads + last))
        def _():
            compute(t - last)

        reduce_step(t - last - z, 1)
        reduce_step(t - 2 * last + z, -1)

        @pl.when((t >= 2 * last) & (t < heads + 2 * last))
        def _():
            finish(t - 2 * last)

    w_local.wait()
    w_remote.wait()

    @pl.loop(0, heads)
    def _(h):
        att_copy(h).wait_recv()

    tile = math.gcd(columns, 512)

    @pl.loop(0, columns // tile)
    def _(n):
        here = pl.ds(pl.multiple_of(n * tile, tile), tile)
        y_ref[:, here] = jnp.dot(
            att[...], wv[:, here], preferred_element_type=jnp.float32
        ).astype(jnp.bfloat16)

    @pl.loop(0, heads)
    def _(h):
        att_copy(h).wait_send()
        for copy in kv_copies(h):
            copy.wait_send()
        for other_z in range(stages):

            @pl.when((other_z <= z) & has_right)
            def _():
                ag_copy(h, other_z, 1).wait_send()

            @pl.when((other_z >= z) & has_left)
            def _():
                ag_copy(h, other_z, -1).wait_send()

            @pl.when(other_z > z)
            def _():
                rs_copy(h, other_z, 1).wait_send()

            @pl.when(other_z < z)
            def _():
                rs_copy(h, other_z, -1).wait_send()


def routed_by_lines(queries, span_keys, span_values, cache_keys, cache_values, routes, out_weight):
    blocks, heads = routes.shape[1:3]
    devices = lax.axis_size("ctx")
    stages = devices // 2
    rows = blocks * QB
    span = cache_keys.shape[0]
    columns = out_weight.shape[1] // lax.axis_size("head")
    named = jnp.any(
        routes[0][None] == jnp.arange(devices, dtype=jnp.int32)[:, None, None, None], axis=-1
    )
    flags = named.transpose(2, 0, 1).reshape(heads, devices * blocks).astype(jnp.bfloat16)
    tail = devices * blocks
    flags = jnp.broadcast_to(flags[:, :, None], (heads, tail, DH))
    vmem = pl.BlockSpec(memory_space=pltpu.VMEM)
    message = (heads, stages, DH + EXTRA, rows)
    dma = pltpu.SemaphoreType.DMA
    return pl.pallas_call(
        functools.partial(kernel, stages, heads, blocks),
        out_shape=jax.ShapeDtypeStruct((rows, columns), jnp.bfloat16),
        in_specs=[vmem] * 6 + [pl.BlockSpec(memory_space=pl.ANY)],
        out_specs=vmem,
        scratch_shapes=[
            pltpu.VMEM((stages, heads, rows + tail, DH), jnp.bfloat16),
            pltpu.VMEM((heads, span, DH), jnp.bfloat16),
            pltpu.VMEM((heads, span, DH), jnp.bfloat16),
            pltpu.VMEM(message, jnp.bfloat16),
            pltpu.VMEM(message, jnp.bfloat16),
            pltpu.VMEM(message, jnp.bfloat16),
            pltpu.VMEM((heads, DH + EXTRA, rows), jnp.bfloat16),
            pltpu.VMEM((rows, 2 * heads * DH), jnp.bfloat16),
            pltpu.VMEM((2 * heads * DH, columns), jnp.bfloat16),
            dma((2, heads, stages)),
            dma((heads, stages)),
            dma((heads, stages)),
            dma((2, heads, stages)),
            dma((2, heads)),
            dma((2, heads)),
            dma((heads,)),
            dma((heads,)),
            dma((3,)),
        ],
        compiler_params=pltpu.CompilerParams(
            collective_id=0, has_side_effects=True, vmem_limit_bytes=60 * 2**20
        ),
        cost_estimate=pl.CostEstimate(
            flops=8 * stages * heads * rows * span * DH, bytes_accessed=2**24, transcendentals=0
        ),
    )(queries, flags, span_keys, span_values, cache_keys, cache_values, out_weight)


def on_device(queries, span_keys, span_values, cache_keys, cache_values, routes, out_weight):
    blocks, heads, top_picks = routes.shape[1:]
    devices = lax.axis_size("ctx")
    arguments = (queries, span_keys, span_values, cache_keys, cache_values, routes, out_weight)
    slots = max(2, 2 * blocks * heads * top_picks // devices)
    dense = slots >= blocks * heads and devices % 2 == 0 and lax.axis_size("head") == 2
    return (routed_by_lines if dense else routed_by_slots)(*arguments)


def solution(mesh):
    placed = (
        P(("groups", "ctx"), "head"),
        P(("groups", "ctx"), "head"),
        P(("groups", "ctx"), "head"),
        P(("groups", "ctx"), "head"),
        P(("groups", "ctx"), "head"),
        P("head", ("groups", "ctx"), None, None),
        P("head", None),
    )
    return jax.shard_map(
        on_device,
        mesh=mesh,
        in_specs=placed,
        out_specs=P(("groups", "ctx"), "head"),
        check_vma=False,
    )
```

```python
import functools
import math

import jax
import jax.numpy as jnp
from jax import lax
from jax.experimental import pallas as pl
from jax.experimental.pallas import tpu as pltpu
from jax.sharding import PartitionSpec as P

DH = 128
QB = 128


def shortened(value):

    def short(part):
        return part.astype(jnp.bfloat16) if part.dtype == jnp.float32 else part

    return jax.tree.map(short, value)


def soft_partial(scores, values_block, pattern):
    highest = jnp.max(scores, axis=-1, keepdims=True)
    exponent = jnp.exp(scores - highest)
    denominator = jnp.sum(exponent, axis=-1, keepdims=True)
    weights_low = (exponent / denominator).astype(jnp.bfloat16)
    result = jnp.einsum(
        pattern, weights_low, values_block, preferred_element_type=jnp.float32
    ).astype(jnp.bfloat16)
    log_total = highest[..., 0] + jnp.log(denominator[..., 0])
    return (result, log_total)


def routed_by_slots(queries, span_keys, span_values, cache_keys, cache_values, routes, out_weight):
    blocks = routes.shape[1]
    heads_here = routes.shape[2]
    top_picks = routes.shape[3]
    key_rows = cache_keys.shape[0]
    devices = lax.axis_size("ctx")
    scaling = 1.0 / math.sqrt(DH)
    blocked = queries.reshape(blocks, QB, heads_here, DH)
    most_rows = max(2, 2 * blocks * heads_here * top_picks // devices)
    groups = 1
    per_peer = groups * most_rows
    slot_total = per_peer * devices
    wanted = routes.reshape(-1)
    item_count = wanted.shape[0]
    item_ids = jnp.arange(item_count, dtype=jnp.int32)
    block_of = item_ids // (heads_here * top_picks)
    head_of = item_ids // top_picks % heads_here
    bucket = wanted * groups + block_of % groups
    one_hot = (bucket[:, None] == jnp.arange(devices * groups, dtype=jnp.int32)[None, :]).astype(
        jnp.int32
    )
    ranking = jnp.sum(jnp.cumsum(one_hot, axis=0) * one_hot, axis=1) - 1
    position = (block_of % groups * most_rows + ranking) * devices + wanted
    matches = position[None, :] == jnp.arange(slot_total, dtype=jnp.int32)[:, None]
    filled = jnp.any(matches, axis=1)
    source = jnp.sum(jnp.where(matches, item_ids[None, :], 0), axis=1)
    gathered = blocked[block_of[source], :, head_of[source], :]
    slot_queries = jnp.where(filled[:, None, None], gathered, jnp.zeros_like(gathered)).reshape(
        per_peer, devices, QB, DH
    )
    slot_heads = jnp.where(filled, head_of[source], 0).reshape(per_peer, devices)
    keys_by_head = cache_keys.reshape(key_rows, heads_here, DH).transpose(1, 0, 2)
    values_by_head = cache_values.reshape(key_rows, heads_here, DH).transpose(1, 0, 2)

    def one_portion(portion):
        queried, head_ids = portion
        chosen_keys = keys_by_head[head_ids]
        chosen_values = values_by_head[head_ids]
        scores = (
            jnp.einsum("pqd,pkd->pqk", queried, chosen_keys, preferred_element_type=jnp.float32)
            * scaling
        )
        return soft_partial(scores, chosen_values, "pqk,pkd->pqd")

    outputs, log_sums = lax.map(
        one_portion,
        (
            lax.all_to_all(slot_queries, "ctx", split_axis=1, concat_axis=1, tiled=True),
            lax.all_to_all(slot_heads, "ctx", split_axis=1, concat_axis=1, tiled=True),
        ),
    )
    outputs_back = jax.tree.map(
        lambda part, own: part.astype(own.dtype),
        lax.all_to_all(shortened(outputs), "ctx", split_axis=1, concat_axis=1, tiled=True),
        outputs,
    )
    sums_back = lax.all_to_all(log_sums, "ctx", split_axis=1, concat_axis=1, tiled=True)
    routed_out = outputs_back.reshape(slot_total, QB, DH)[position].reshape(
        blocks, heads_here, top_picks, QB, DH
    )
    routed_lse = sums_back.reshape(slot_total, QB)[position].reshape(
        blocks, heads_here, top_picks, QB
    )
    own_keys = span_keys.reshape(blocks, QB, heads_here, DH)
    own_values = span_values.reshape(blocks, QB, heads_here, DH)
    causal = jnp.arange(QB)[:, None] >= jnp.arange(QB)[None, :]
    self_scores = (
        jnp.einsum("bqhd,bkhd->bhqk", blocked, own_keys, preferred_element_type=jnp.float32)
        * scaling
    )
    self_scores = jnp.where(causal[None, None], self_scores, -jnp.inf)
    self_out, self_lse = soft_partial(self_scores, own_values, "bhqk,bkhd->bhqd")
    all_lse = jnp.concatenate([routed_lse, self_lse[:, :, None]], axis=2)
    all_out = jnp.concatenate(
        [routed_out.astype(jnp.float32), self_out[:, :, None].astype(jnp.float32)], axis=2
    )
    highest = jnp.max(all_lse, axis=2, keepdims=True)
    merge_weights = jnp.exp(all_lse - highest)
    merge_weights = merge_weights / jnp.sum(merge_weights, axis=2, keepdims=True)
    attention = jnp.sum(merge_weights[..., None] * all_out, axis=2)
    attention = (
        attention.transpose(0, 2, 1, 3).reshape(blocks * QB, heads_here * DH).astype(jnp.bfloat16)
    )
    partial_sums = jnp.dot(attention, out_weight, preferred_element_type=jnp.float32)
    return lax.psum_scatter(partial_sums, "head", scatter_dimension=1, tiled=True).astype(
        jnp.bfloat16
    )


BIG = 1e30
LOG2E = math.log2(math.e)
LANES = 128
VALUE_ROWS = DH + 16


def store_partial(ref, lse_ref, out, lse):
    ref[...] = out.astype(jnp.bfloat16)
    lse_ref[...] = lse


def load_partial(ref, lse_ref):
    return ref[...].astype(jnp.float32), lse_ref[...]


def merged(first, second):
    out_a, lse_a = first
    out_b, lse_b = second
    top = jnp.maximum(lse_a, lse_b)
    weight_a = jnp.exp2(lse_a - top)
    weight_b = jnp.exp2(lse_b - top)
    total = weight_a + weight_b
    return (
        out_a * (weight_a / total) + out_b * (weight_b / total),
        top + jnp.log2(total),
    )


def kernel(
    stages,
    heads,
    blocks,
    q_ref,
    flag_ref,
    span_k,
    span_v,
    k_ref,
    v_ref,
    w_hbm,
    y_ref,
    qg,
    kr,
    vr,
    fg,
    chosen_rows,
    part,
    part_lse,
    arrived,
    arrived_lse,
    selfp,
    self_lse,
    vt,
    att,
    wv,
    ag_send,
    ag_recv,
    flag_send,
    flag_recv,
    rs_send,
    rs_recv,
    lse_send,
    lse_recv,
    kv_send,
    kv_recv,
    att_send,
    att_recv,
    w_sem,
):
    rows = blocks * QB
    span = k_ref.shape[0]
    width = heads * DH
    columns = y_ref.shape[1]
    me = lax.axis_index("ctx")
    core = lax.axis_index("head")
    z = me // 2
    y = me % 2
    pair = me + 1 - 2 * y
    other = 1 - core
    last = stages - 1
    has_left = z > 0
    has_right = z < stages - 1
    scale = LOG2E / math.sqrt(DH)

    def head_columns(h):
        return pl.ds(pl.multiple_of(h * DH, DH), DH)

    barrier = pltpu.get_barrier_semaphore()
    pl.semaphore_signal(barrier, inc=1, device_id={"ctx": pair})
    pl.semaphore_signal(barrier, inc=1, device_id={"head": other})

    @pl.when(has_left)
    def _():
        pl.semaphore_signal(barrier, inc=1, device_id={"ctx": me - 2})

    @pl.when(has_right)
    def _():
        pl.semaphore_signal(barrier, inc=1, device_id={"ctx": me + 2})

    for h in range(heads):
        qg[z, h] = q_ref[:, h * DH : (h + 1) * DH]
    fg[z] = flag_ref[...]

    pl.semaphore_wait(
        barrier, 2 + jnp.minimum(z, 1) + jnp.minimum(stages - 1 - z, 1)
    )

    def kv_copies(h):
        return (
            pltpu.make_async_remote_copy(
                src_ref=k_ref.at[:, head_columns(h)],
                dst_ref=kr.at[h],
                send_sem=kv_send.at[0, h],
                recv_sem=kv_recv.at[0, h],
                device_id={"ctx": pair},
            ),
            pltpu.make_async_remote_copy(
                src_ref=v_ref.at[:, head_columns(h)],
                dst_ref=vr.at[h],
                send_sem=kv_send.at[1, h],
                recv_sem=kv_recv.at[1, h],
                device_id={"ctx": pair},
            ),
        )

    def ag_copy(h, source, step):
        return pltpu.make_async_remote_copy(
            src_ref=qg.at[source, h],
            dst_ref=qg.at[source, h],
            send_sem=ag_send.at[(step + 1) // 2, h, source],
            recv_sem=ag_recv.at[h, source],
            device_id={"ctx": me + 2 * step},
        )

    def flag_copy(source, step):
        return pltpu.make_async_remote_copy(
            src_ref=fg.at[source],
            dst_ref=fg.at[source],
            send_sem=flag_send.at[(step + 1) // 2, source],
            recv_sem=flag_recv.at[source],
            device_id={"ctx": me + 2 * step},
        )

    def rs_copies(h, dest, step):
        side = (step + 1) // 2
        return (
            pltpu.make_async_remote_copy(
                src_ref=part.at[h, dest],
                dst_ref=arrived.at[side, h, dest],
                send_sem=rs_send.at[h, dest],
                recv_sem=rs_recv.at[side, h, dest],
                device_id={"ctx": me + 2 * step},
            ),
            pltpu.make_async_remote_copy(
                src_ref=part_lse.at[h, dest],
                dst_ref=arrived_lse.at[side, h, dest],
                send_sem=lse_send.at[h, dest],
                recv_sem=lse_recv.at[side, h, dest],
                device_id={"ctx": me + 2 * step},
            ),
        )

    def att_copy(h):
        place = pl.ds(pl.multiple_of(core * width + h * DH, DH), DH)
        return pltpu.make_async_remote_copy(
            src_ref=att.at[:, place],
            dst_ref=att.at[:, place],
            send_sem=att_send.at[h],
            recv_sem=att_recv.at[h],
            device_id={"head": other},
        )

    w_rows = pl.ds(pl.multiple_of(core * width, DH), width)
    w_remote = pltpu.make_async_remote_copy(
        src_ref=w_hbm.at[:, pl.ds(pl.multiple_of(other * columns, DH), columns)],
        dst_ref=wv.at[w_rows, :],
        send_sem=w_sem.at[0],
        recv_sem=w_sem.at[1],
        device_id={"head": other},
    )
    w_local = pltpu.make_async_copy(
        w_hbm.at[:, pl.ds(pl.multiple_of(core * columns, DH), columns)],
        wv.at[w_rows, :],
        w_sem.at[2],
    )

    def lead(step):
        return 2 * (last - z if step > 0 else z)

    def send_own(h, step):
        onward = has_right if step > 0 else has_left

        @pl.when((h < heads) & onward)
        def _():
            ag_copy(h, z, step).start()

        @pl.when((h == 0) & onward)
        def _():
            flag_copy(z, step).start()

    def gather_step(t):
        for step in (1, -1):
            send_own(t + lead(step), step)
        for a in range(1, stages):
            h = t - a

            @pl.when((h >= 0) & (h < heads))
            def _():
                for step in (1, -1):
                    source = z - a * step
                    here = (source >= 0) & (source < stages)
                    onward = has_right if step > 0 else has_left

                    @pl.when(here)
                    def _():
                        ag_copy(h, source, step).wait_recv()

                        @pl.when(onward)
                        def _():
                            ag_copy(h, source, step).start()

                        @pl.when(h == 0)
                        def _():
                            flag_copy(source, step).wait_recv()

                            @pl.when(onward)
                            def _():
                                flag_copy(source, step).start()

    def read_flags():
        for s in range(stages):
            flags = fg[s].astype(jnp.float32)
            lane = lax.broadcasted_iota(jnp.int32, flags.shape, 1)
            for at, number in enumerate((me, pair)):
                chosen = jnp.sum(
                    jnp.where(lane == number, flags, 0.0), axis=1, keepdims=True
                )
                chosen_rows[s, at] = jnp.broadcast_to(chosen, flags.shape)

    def prepare(h):
        for copy in kv_copies(h):
            copy.wait_recv()
        filler = jnp.ones((VALUE_ROWS - DH, span), jnp.bfloat16)
        for at, value in enumerate((v_ref[:, head_columns(h)], vr[h])):
            vt[at, 0:DH, :] = value.T
            vt[at, DH:VALUE_ROWS, :] = filler

    def compute(h, s):
        keys = (k_ref.at[:, head_columns(h)], kr.at[h])
        queried = qg[s, h]
        routed, scores, highest = [], [], None
        for at in range(2):
            chosen = jnp.concatenate(
                [chosen_rows[s, at, pl.ds(h * blocks + j, 1), :] for j in range(blocks)],
                axis=1,
            )
            score = lax.dot_general(
                keys[at][...],
                queried,
                (((1,), (1,)), ((), ())),
                preferred_element_type=jnp.float32,
            )
            top = jnp.where(
                chosen > 0.0, jnp.max(score, axis=0, keepdims=True) * scale, -BIG
            )
            highest = top if highest is None else jnp.maximum(highest, top)
            routed.append(chosen)
            scores.append(score)
        result = None
        for at in range(2):
            shift = jnp.where(routed[at] > 0.0, highest, BIG)
            exponent = jnp.exp2(scores[at] * scale - shift).astype(jnp.bfloat16)
            product = jnp.dot(vt[at], exponent, preferred_element_type=jnp.float32)
            result = product if result is None else result + product
        total = result[DH : DH + 1, :]
        safe = jnp.maximum(total, 0.5)
        store_partial(
            part.at[h, s],
            part_lse.at[h, s],
            result[0:DH, :] * (1.0 / safe),
            jnp.where(total > 0.0, highest + jnp.log2(safe), -BIG),
        )

    def self_part(h):
        for j in range(blocks):
            here = pl.ds(j * QB, QB)
            score = lax.dot_general(
                span_k[here, head_columns(h)],
                q_ref[here, head_columns(h)],
                (((1,), (1,)), ((), ())),
                preferred_element_type=jnp.float32,
            )
            shape = (QB, QB)
            causal = lax.broadcasted_iota(jnp.int32, shape, 0) <= lax.broadcasted_iota(
                jnp.int32, shape, 1
            )
            score = jnp.where(causal, score * scale, -BIG)
            top = jnp.max(score, axis=0, keepdims=True)
            exponent = jnp.exp2(score - top)
            total = jnp.sum(exponent, axis=0, keepdims=True)
            out = jnp.dot(
                span_v[here, head_columns(h)].T,
                exponent.astype(jnp.bfloat16),
                preferred_element_type=jnp.float32,
            )
            store_partial(
                selfp.at[h, :, j * QB : (j + 1) * QB],
                self_lse.at[h, :, j * QB : (j + 1) * QB],
                out * (1.0 / total),
                top + jnp.log2(total),
            )

    def reduce_step(h, step):
        side = (step + 1) // 2
        first = ~has_left if step > 0 else ~has_right

        @pl.when((h >= 0) & (h < heads))
        def _():
            for dest in reversed(range(stages)) if step > 0 else range(stages):
                ahead = (dest - z) * step

                @pl.when((ahead >= 0) & ~first)
                def _():
                    for copy in rs_copies(h, dest, step):
                        copy.wait_recv()
                    mine = (part.at[h, dest], part_lse.at[h, dest])
                    store_partial(
                        *mine,
                        *merged(
                            load_partial(*mine),
                            load_partial(
                                arrived.at[side, h, dest], arrived_lse.at[side, h, dest]
                            ),
                        ),
                    )

                @pl.when(ahead > 0)
                def _():
                    for copy in rs_copies(h, dest, step):
                        copy.start()

    def finish(h):
        out, _ = merged(
            load_partial(part.at[h, z], part_lse.at[h, z]),
            load_partial(selfp.at[h], self_lse.at[h]),
        )
        place = pl.ds(pl.multiple_of(core * width + h * DH, DH), DH)
        att[:, place] = out.T.astype(jnp.bfloat16)
        att_copy(h).start()

    for step in (1, -1):

        @pl.loop(0, lead(step) + 1)
        def _(h):
            send_own(h, step)

    @pl.loop(0, heads)
    def _(h):
        for copy in kv_copies(h):
            copy.start()

    w_remote.start()
    w_local.start()

    @pl.loop(0, heads)
    def _(h):
        self_part(h)

    @pl.loop(1, heads + 2 * last + 1)
    def _(t):
        gather_step(t)
        h = t - last
        busy = (h >= 0) & (h < heads)

        @pl.when(h == 0)
        def _():
            read_flags()

        @pl.when(busy)
        def _():
            prepare(h)
            for s in range(stages):
                compute(h, s)

        reduce_step(h - z, 1)
        reduce_step(h - last + z, -1)

        @pl.when((h >= last) & (h < heads + last))
        def _():
            finish(h - last)

    w_local.wait()
    w_remote.wait()

    @pl.loop(0, heads)
    def _(h):
        att_copy(h).wait_recv()

    tile = math.gcd(columns, 512)

    @pl.loop(0, columns // tile)
    def _(n):
        here = pl.ds(pl.multiple_of(n * tile, tile), tile)
        y_ref[:, here] = jnp.dot(
            att[...], wv[:, here], preferred_element_type=jnp.float32
        ).astype(jnp.bfloat16)

    @pl.loop(0, heads)
    def _(h):
        att_copy(h).wait_send()
        for copy in kv_copies(h):
            copy.wait_send()
        for other_z in range(stages):

            @pl.when((other_z <= z) & has_right)
            def _():
                ag_copy(h, other_z, 1).wait_send()

            @pl.when((other_z >= z) & has_left)
            def _():
                ag_copy(h, other_z, -1).wait_send()

            for step in (1, -1):

                @pl.when((other_z - z) * step > 0)
                def _():
                    for copy in rs_copies(h, other_z, step):
                        copy.wait_send()

    for other_z in range(stages):

        @pl.when((other_z <= z) & has_right)
        def _():
            flag_copy(other_z, 1).wait_send()

        @pl.when((other_z >= z) & has_left)
        def _():
            flag_copy(other_z, -1).wait_send()


def routed_by_lines(queries, span_keys, span_values, cache_keys, cache_values, routes, out_weight):
    blocks, heads = routes.shape[1:3]
    devices = lax.axis_size("ctx")
    stages = devices // 2
    rows = blocks * QB
    span = cache_keys.shape[0]
    columns = out_weight.shape[1] // lax.axis_size("head")
    named = jnp.any(
        routes[0][None] == jnp.arange(devices, dtype=jnp.int32)[:, None, None, None], axis=-1
    )
    flags = named.transpose(2, 1, 0).reshape(heads * blocks, devices).astype(jnp.bfloat16)
    flags = jnp.pad(flags, ((0, 0), (0, LANES - devices)))
    vmem = pl.BlockSpec(memory_space=pltpu.VMEM)
    dma = pltpu.SemaphoreType.DMA
    return pl.pallas_call(
        functools.partial(kernel, stages, heads, blocks),
        out_shape=jax.ShapeDtypeStruct((rows, columns), jnp.bfloat16),
        in_specs=[vmem] * 6 + [pl.BlockSpec(memory_space=pl.ANY)],
        out_specs=vmem,
        scratch_shapes=[
            pltpu.VMEM((stages, heads, rows, DH), jnp.bfloat16),
            pltpu.VMEM((heads, span, DH), jnp.bfloat16),
            pltpu.VMEM((heads, span, DH), jnp.bfloat16),
            pltpu.VMEM((stages, heads * blocks, LANES), jnp.bfloat16),
            pltpu.VMEM((stages, 2, heads * blocks, LANES), jnp.float32),
            pltpu.VMEM((heads, stages, DH, rows), jnp.bfloat16),
            pltpu.VMEM((heads, stages, 1, rows), jnp.float32),
            pltpu.VMEM((2, heads, stages, DH, rows), jnp.bfloat16),
            pltpu.VMEM((2, heads, stages, 1, rows), jnp.float32),
            pltpu.VMEM((heads, DH, rows), jnp.bfloat16),
            pltpu.VMEM((heads, 1, rows), jnp.float32),
            pltpu.VMEM((2, VALUE_ROWS, span), jnp.bfloat16),
            pltpu.VMEM((rows, 2 * heads * DH), jnp.bfloat16),
            pltpu.VMEM((2 * heads * DH, columns), jnp.bfloat16),
            dma((2, heads, stages)),
            dma((heads, stages)),
            dma((2, stages)),
            dma((stages,)),
            dma((heads, stages)),
            dma((2, heads, stages)),
            dma((heads, stages)),
            dma((2, heads, stages)),
            dma((2, heads)),
            dma((2, heads)),
            dma((heads,)),
            dma((heads,)),
            dma((3,)),
        ],
        compiler_params=pltpu.CompilerParams(
            collective_id=0, has_side_effects=True, vmem_limit_bytes=60 * 2**20
        ),
        cost_estimate=pl.CostEstimate(
            flops=8 * stages * heads * rows * span * DH, bytes_accessed=2**24, transcendentals=0
        ),
    )(queries, flags, span_keys, span_values, cache_keys, cache_values, out_weight)


def on_device(queries, span_keys, span_values, cache_keys, cache_values, routes, out_weight):
    blocks, heads, top_picks = routes.shape[1:]
    devices = lax.axis_size("ctx")
    arguments = (queries, span_keys, span_values, cache_keys, cache_values, routes, out_weight)
    slots = max(2, 2 * blocks * heads * top_picks // devices)
    dense = slots >= blocks * heads and devices % 2 == 0 and devices <= LANES and lax.axis_size("head") == 2
    return (routed_by_lines if dense else routed_by_slots)(*arguments)


def solution(mesh):
    placed = (
        P(("groups", "ctx"), "head"),
        P(("groups", "ctx"), "head"),
        P(("groups", "ctx"), "head"),
        P(("groups", "ctx"), "head"),
        P(("groups", "ctx"), "head"),
        P("head", ("groups", "ctx"), None, None),
        P("head", None),
    )
    return jax.shard_map(
        on_device,
        mesh=mesh,
        in_specs=placed,
        out_specs=P(("groups", "ctx"), "head"),
        check_vma=False,
    )
```

```python
import functools
import math

import jax
import jax.numpy as jnp
from jax import lax
from jax.experimental import pallas as pl
from jax.experimental.pallas import tpu as pltpu
from jax.sharding import PartitionSpec as P

DH = 128
QB = 128


def shortened(value):

    def short(part):
        return part.astype(jnp.bfloat16) if part.dtype == jnp.float32 else part

    return jax.tree.map(short, value)


def soft_partial(scores, values_block, pattern):
    highest = jnp.max(scores, axis=-1, keepdims=True)
    exponent = jnp.exp(scores - highest)
    denominator = jnp.sum(exponent, axis=-1, keepdims=True)
    weights_low = (exponent / denominator).astype(jnp.bfloat16)
    result = jnp.einsum(
        pattern, weights_low, values_block, preferred_element_type=jnp.float32
    ).astype(jnp.bfloat16)
    log_total = highest[..., 0] + jnp.log(denominator[..., 0])
    return (result, log_total)


def routed_by_slots(queries, span_keys, span_values, cache_keys, cache_values, routes, out_weight):
    blocks = routes.shape[1]
    heads_here = routes.shape[2]
    top_picks = routes.shape[3]
    key_rows = cache_keys.shape[0]
    devices = lax.axis_size("ctx")
    scaling = 1.0 / math.sqrt(DH)
    blocked = queries.reshape(blocks, QB, heads_here, DH)
    most_rows = max(2, 2 * blocks * heads_here * top_picks // devices)
    groups = 1
    per_peer = groups * most_rows
    slot_total = per_peer * devices
    wanted = routes.reshape(-1)
    item_count = wanted.shape[0]
    item_ids = jnp.arange(item_count, dtype=jnp.int32)
    block_of = item_ids // (heads_here * top_picks)
    head_of = item_ids // top_picks % heads_here
    bucket = wanted * groups + block_of % groups
    one_hot = (bucket[:, None] == jnp.arange(devices * groups, dtype=jnp.int32)[None, :]).astype(
        jnp.int32
    )
    ranking = jnp.sum(jnp.cumsum(one_hot, axis=0) * one_hot, axis=1) - 1
    position = (block_of % groups * most_rows + ranking) * devices + wanted
    matches = position[None, :] == jnp.arange(slot_total, dtype=jnp.int32)[:, None]
    filled = jnp.any(matches, axis=1)
    source = jnp.sum(jnp.where(matches, item_ids[None, :], 0), axis=1)
    gathered = blocked[block_of[source], :, head_of[source], :]
    slot_queries = jnp.where(filled[:, None, None], gathered, jnp.zeros_like(gathered)).reshape(
        per_peer, devices, QB, DH
    )
    slot_heads = jnp.where(filled, head_of[source], 0).reshape(per_peer, devices)
    keys_by_head = cache_keys.reshape(key_rows, heads_here, DH).transpose(1, 0, 2)
    values_by_head = cache_values.reshape(key_rows, heads_here, DH).transpose(1, 0, 2)

    def one_portion(portion):
        queried, head_ids = portion
        chosen_keys = keys_by_head[head_ids]
        chosen_values = values_by_head[head_ids]
        scores = (
            jnp.einsum("pqd,pkd->pqk", queried, chosen_keys, preferred_element_type=jnp.float32)
            * scaling
        )
        return soft_partial(scores, chosen_values, "pqk,pkd->pqd")

    outputs, log_sums = lax.map(
        one_portion,
        (
            lax.all_to_all(slot_queries, "ctx", split_axis=1, concat_axis=1, tiled=True),
            lax.all_to_all(slot_heads, "ctx", split_axis=1, concat_axis=1, tiled=True),
        ),
    )
    outputs_back = jax.tree.map(
        lambda part, own: part.astype(own.dtype),
        lax.all_to_all(shortened(outputs), "ctx", split_axis=1, concat_axis=1, tiled=True),
        outputs,
    )
    sums_back = lax.all_to_all(log_sums, "ctx", split_axis=1, concat_axis=1, tiled=True)
    routed_out = outputs_back.reshape(slot_total, QB, DH)[position].reshape(
        blocks, heads_here, top_picks, QB, DH
    )
    routed_lse = sums_back.reshape(slot_total, QB)[position].reshape(
        blocks, heads_here, top_picks, QB
    )
    own_keys = span_keys.reshape(blocks, QB, heads_here, DH)
    own_values = span_values.reshape(blocks, QB, heads_here, DH)
    causal = jnp.arange(QB)[:, None] >= jnp.arange(QB)[None, :]
    self_scores = (
        jnp.einsum("bqhd,bkhd->bhqk", blocked, own_keys, preferred_element_type=jnp.float32)
        * scaling
    )
    self_scores = jnp.where(causal[None, None], self_scores, -jnp.inf)
    self_out, self_lse = soft_partial(self_scores, own_values, "bhqk,bkhd->bhqd")
    all_lse = jnp.concatenate([routed_lse, self_lse[:, :, None]], axis=2)
    all_out = jnp.concatenate(
        [routed_out.astype(jnp.float32), self_out[:, :, None].astype(jnp.float32)], axis=2
    )
    highest = jnp.max(all_lse, axis=2, keepdims=True)
    merge_weights = jnp.exp(all_lse - highest)
    merge_weights = merge_weights / jnp.sum(merge_weights, axis=2, keepdims=True)
    attention = jnp.sum(merge_weights[..., None] * all_out, axis=2)
    attention = (
        attention.transpose(0, 2, 1, 3).reshape(blocks * QB, heads_here * DH).astype(jnp.bfloat16)
    )
    partial_sums = jnp.dot(attention, out_weight, preferred_element_type=jnp.float32)
    return lax.psum_scatter(partial_sums, "head", scatter_dimension=1, tiled=True).astype(
        jnp.bfloat16
    )


BIG = 1e30
LOG2E = math.log2(math.e)
LANES = 128
VALUE_ROWS = DH + 16


def store_partial(ref, lse_ref, out, lse):
    ref[...] = out.astype(jnp.bfloat16)
    lse_ref[...] = lse


def load_partial(ref, lse_ref):
    return ref[...].astype(jnp.float32), lse_ref[...]


def merged(first, second):
    out_a, lse_a = first
    out_b, lse_b = second
    top = jnp.maximum(lse_a, lse_b)
    weight_a = jnp.exp2(lse_a - top)
    weight_b = jnp.exp2(lse_b - top)
    total = weight_a + weight_b
    return (
        out_a * (weight_a / total) + out_b * (weight_b / total),
        top + jnp.log2(total),
    )


def kernel(
    stages,
    heads,
    blocks,
    q_hbm,
    flag_ref,
    span_k_hbm,
    span_v_hbm,
    k_hbm,
    v_hbm,
    w_hbm,
    y_ref,
    qg,
    kr,
    vr,
    fg,
    chosen_rows,
    part,
    part_lse,
    arrived,
    arrived_lse,
    selfp,
    self_lse,
    vt,
    att,
    wv,
    span_k,
    span_v,
    k_ref,
    v_ref,
    ag_send,
    ag_recv,
    flag_send,
    flag_recv,
    rs_send,
    rs_recv,
    lse_send,
    lse_recv,
    kv_send,
    kv_recv,
    att_send,
    att_recv,
    w_sem,
    own_sem,
    q_sem,
):
    rows = blocks * QB
    span = k_ref.shape[0]
    width = heads * DH
    columns = y_ref.shape[1]
    me = lax.axis_index("ctx")
    core = lax.axis_index("head")
    z = me // 2
    y = me % 2
    pair = me + 1 - 2 * y
    other = 1 - core
    last = stages - 1
    has_left = z > 0
    has_right = z < stages - 1
    scale = LOG2E / math.sqrt(DH)

    def head_columns(h):
        return pl.ds(pl.multiple_of(h * DH, DH), DH)

    barrier = pltpu.get_barrier_semaphore()
    pl.semaphore_signal(barrier, inc=1, device_id={"ctx": pair})
    pl.semaphore_signal(barrier, inc=1, device_id={"head": other})

    @pl.when(has_left)
    def _():
        pl.semaphore_signal(barrier, inc=1, device_id={"ctx": me - 2})

    @pl.when(has_right)
    def _():
        pl.semaphore_signal(barrier, inc=1, device_id={"ctx": me + 2})

    fg[z] = flag_ref[...]

    pl.semaphore_wait(
        barrier, 2 + jnp.minimum(z, 1) + jnp.minimum(stages - 1 - z, 1)
    )

    def kv_copies(h):
        return (
            pltpu.make_async_remote_copy(
                src_ref=k_hbm.at[:, head_columns(h)],
                dst_ref=kr.at[h],
                send_sem=kv_send.at[0, h],
                recv_sem=kv_recv.at[0, h],
                device_id={"ctx": pair},
            ),
            pltpu.make_async_remote_copy(
                src_ref=v_hbm.at[:, head_columns(h)],
                dst_ref=vr.at[h],
                send_sem=kv_send.at[1, h],
                recv_sem=kv_recv.at[1, h],
                device_id={"ctx": pair},
            ),
        )

    def q_copy(h):
        return pltpu.make_async_copy(q_hbm.at[:, head_columns(h)], qg.at[z, h], q_sem.at[h])

    own_copies = [
        pltpu.make_async_copy(source, target, own_sem.at[i])
        for i, (source, target) in enumerate(
            ((k_hbm, k_ref), (v_hbm, v_ref), (span_k_hbm, span_k), (span_v_hbm, span_v))
        )
    ]

    def ag_copy(h, source, step, own=False):
        return pltpu.make_async_remote_copy(
            src_ref=q_hbm.at[:, head_columns(h)] if own else qg.at[source, h],
            dst_ref=qg.at[source, h],
            send_sem=ag_send.at[(step + 1) // 2, h, source],
            recv_sem=ag_recv.at[h, source],
            device_id={"ctx": me + 2 * step},
        )

    def flag_copy(source, step):
        return pltpu.make_async_remote_copy(
            src_ref=fg.at[source],
            dst_ref=fg.at[source],
            send_sem=flag_send.at[(step + 1) // 2, source],
            recv_sem=flag_recv.at[source],
            device_id={"ctx": me + 2 * step},
        )

    def rs_copies(h, dest, step):
        side = (step + 1) // 2
        return (
            pltpu.make_async_remote_copy(
                src_ref=part.at[h, dest],
                dst_ref=arrived.at[side, h, dest],
                send_sem=rs_send.at[h, dest],
                recv_sem=rs_recv.at[side, h, dest],
                device_id={"ctx": me + 2 * step},
            ),
            pltpu.make_async_remote_copy(
                src_ref=part_lse.at[h, dest],
                dst_ref=arrived_lse.at[side, h, dest],
                send_sem=lse_send.at[h, dest],
                recv_sem=lse_recv.at[side, h, dest],
                device_id={"ctx": me + 2 * step},
            ),
        )

    def att_copy(h):
        place = pl.ds(pl.multiple_of(core * width + h * DH, DH), DH)
        return pltpu.make_async_remote_copy(
            src_ref=att.at[:, place],
            dst_ref=att.at[:, place],
            send_sem=att_send.at[h],
            recv_sem=att_recv.at[h],
            device_id={"head": other},
        )

    w_rows = pl.ds(pl.multiple_of(core * width, DH), width)
    w_remote = pltpu.make_async_remote_copy(
        src_ref=w_hbm.at[:, pl.ds(pl.multiple_of(other * columns, DH), columns)],
        dst_ref=wv.at[w_rows, :],
        send_sem=w_sem.at[0],
        recv_sem=w_sem.at[1],
        device_id={"head": other},
    )
    w_local = pltpu.make_async_copy(
        w_hbm.at[:, pl.ds(pl.multiple_of(core * columns, DH), columns)],
        wv.at[w_rows, :],
        w_sem.at[2],
    )

    def lead(step):
        return 2 * (last - z if step > 0 else z)

    def send_own(h, step):
        onward = has_right if step > 0 else has_left

        @pl.when((h < heads) & onward)
        def _():
            ag_copy(h, z, step, own=True).start()

        @pl.when((h == 0) & onward)
        def _():
            flag_copy(z, step).start()

    def gather_step(t):
        for step in (1, -1):
            send_own(t + lead(step), step)
        for a in range(1, stages):
            h = t - a

            @pl.when((h >= 0) & (h < heads))
            def _():
                for step in (1, -1):
                    source = z - a * step
                    here = (source >= 0) & (source < stages)
                    onward = has_right if step > 0 else has_left

                    @pl.when(here)
                    def _():
                        ag_copy(h, source, step).wait_recv()

                        @pl.when(onward)
                        def _():
                            ag_copy(h, source, step).start()

                        @pl.when(h == 0)
                        def _():
                            flag_copy(source, step).wait_recv()

                            @pl.when(onward)
                            def _():
                                flag_copy(source, step).start()

    def read_flags():
        for s in range(stages):
            flags = fg[s].astype(jnp.float32)
            lane = lax.broadcasted_iota(jnp.int32, flags.shape, 1)
            for at, number in enumerate((me, pair)):
                chosen = jnp.sum(
                    jnp.where(lane == number, flags, 0.0), axis=1, keepdims=True
                )
                chosen_rows[s, at] = jnp.broadcast_to(chosen, flags.shape)

    def prepare(h):
        for copy in kv_copies(h):
            copy.wait_recv()
        filler = jnp.ones((VALUE_ROWS - DH, span), jnp.bfloat16)
        for at, value in enumerate((v_ref[:, head_columns(h)], vr[h])):
            vt[at, 0:DH, :] = value.T
            vt[at, DH:VALUE_ROWS, :] = filler

    def compute(h, s):
        keys = (k_ref.at[:, head_columns(h)], kr.at[h])
        queried = qg[s, h]
        routed, scores, highest = [], [], None
        for at in range(2):
            chosen = jnp.concatenate(
                [chosen_rows[s, at, pl.ds(h * blocks + j, 1), :] for j in range(blocks)],
                axis=1,
            )
            score = lax.dot_general(
                keys[at][...],
                queried,
                (((1,), (1,)), ((), ())),
                preferred_element_type=jnp.float32,
            )
            top = jnp.where(
                chosen > 0.0, jnp.max(score, axis=0, keepdims=True) * scale, -BIG
            )
            highest = top if highest is None else jnp.maximum(highest, top)
            routed.append(chosen)
            scores.append(score)
        result = None
        for at in range(2):
            shift = jnp.where(routed[at] > 0.0, highest, BIG)
            exponent = jnp.exp2(scores[at] * scale - shift).astype(jnp.bfloat16)
            product = jnp.dot(vt[at], exponent, preferred_element_type=jnp.float32)
            result = product if result is None else result + product
        total = result[DH : DH + 1, :]
        safe = jnp.maximum(total, 0.5)
        store_partial(
            part.at[h, s],
            part_lse.at[h, s],
            result[0:DH, :] * (1.0 / safe),
            jnp.where(total > 0.0, highest + jnp.log2(safe), -BIG),
        )

    def self_part(h):
        for j in range(blocks):
            here = pl.ds(j * QB, QB)
            score = lax.dot_general(
                span_k[here, head_columns(h)],
                qg[z, h, here, :],
                (((1,), (1,)), ((), ())),
                preferred_element_type=jnp.float32,
            )
            shape = (QB, QB)
            causal = lax.broadcasted_iota(jnp.int32, shape, 0) <= lax.broadcasted_iota(
                jnp.int32, shape, 1
            )
            score = jnp.where(causal, score * scale, -BIG)
            top = jnp.max(score, axis=0, keepdims=True)
            exponent = jnp.exp2(score - top)
            total = jnp.sum(exponent, axis=0, keepdims=True)
            out = jnp.dot(
                span_v[here, head_columns(h)].T,
                exponent.astype(jnp.bfloat16),
                preferred_element_type=jnp.float32,
            )
            store_partial(
                selfp.at[h, :, j * QB : (j + 1) * QB],
                self_lse.at[h, :, j * QB : (j + 1) * QB],
                out * (1.0 / total),
                top + jnp.log2(total),
            )

    def at_end(step):
        return ~has_left if step > 0 else ~has_right

    def reduce_step(h, step):
        side = (step + 1) // 2

        @pl.when((h >= 0) & (h < heads) & ~at_end(step))
        def _():
            for dest in reversed(range(stages)) if step > 0 else range(stages):
                ahead = (dest - z) * step

                @pl.when(ahead >= 0)
                def _():
                    for copy in rs_copies(h, dest, step):
                        copy.wait_recv()
                    mine = (part.at[h, dest], part_lse.at[h, dest])
                    store_partial(
                        *mine,
                        *merged(
                            load_partial(*mine),
                            load_partial(
                                arrived.at[side, h, dest], arrived_lse.at[side, h, dest]
                            ),
                        ),
                    )

                @pl.when(ahead > 0)
                def _():
                    for copy in rs_copies(h, dest, step):
                        copy.start()

    def finish(h):
        out, _ = merged(
            load_partial(part.at[h, z], part_lse.at[h, z]),
            load_partial(selfp.at[h], self_lse.at[h]),
        )
        place = pl.ds(pl.multiple_of(core * width + h * DH, DH), DH)
        att[:, place] = out.T.astype(jnp.bfloat16)
        att_copy(h).start()

    for step in (1, -1):

        @pl.loop(0, lead(step) + 1)
        def _(h):
            send_own(h, step)

    @pl.loop(0, heads)
    def _(h):
        for copy in kv_copies(h):
            copy.start()

    w_remote.start()
    w_local.start()

    @pl.loop(0, heads)
    def _(h):
        q_copy(h).start()

    for copy in own_copies:
        copy.start()

    @pl.loop(0, heads)
    def _(h):
        q_copy(h).wait()

    @pl.loop(1, heads + 2 * last + 1)
    def _(t):
        gather_step(t)
        h = t - last
        busy = (h >= 0) & (h < heads)

        @pl.when(h == 0)
        def _():
            read_flags()
            for copy in own_copies:
                copy.wait()

        @pl.when(busy)
        def _():
            prepare(h)
            for i in range(stages):
                s = jnp.where(2 * z >= stages, i, last - i)
                compute(h, s)
                for step in (1, -1):

                    @pl.when(((s - z) * step > 0) & at_end(step))
                    def _():
                        for copy in rs_copies(h, s, step):
                            copy.start()

        reduce_step(h - z, 1)
        reduce_step(h - last + z, -1)

        @pl.when(busy)
        def _():
            self_part(h)

        @pl.when((h >= last) & (h < heads + last))
        def _():
            finish(h - last)

    w_local.wait()
    w_remote.wait()

    @pl.loop(0, heads)
    def _(h):
        att_copy(h).wait_recv()

    tile = math.gcd(columns, 512)

    @pl.loop(0, columns // tile)
    def _(n):
        here = pl.ds(pl.multiple_of(n * tile, tile), tile)
        y_ref[:, here] = jnp.dot(
            att[...], wv[:, here], preferred_element_type=jnp.float32
        ).astype(jnp.bfloat16)

    @pl.loop(0, heads)
    def _(h):
        att_copy(h).wait_send()
        for copy in kv_copies(h):
            copy.wait_send()
        for other_z in range(stages):

            @pl.when((other_z <= z) & has_right)
            def _():
                ag_copy(h, other_z, 1).wait_send()

            @pl.when((other_z >= z) & has_left)
            def _():
                ag_copy(h, other_z, -1).wait_send()

            for step in (1, -1):

                @pl.when((other_z - z) * step > 0)
                def _():
                    for copy in rs_copies(h, other_z, step):
                        copy.wait_send()

    for other_z in range(stages):

        @pl.when((other_z <= z) & has_right)
        def _():
            flag_copy(other_z, 1).wait_send()

        @pl.when((other_z >= z) & has_left)
        def _():
            flag_copy(other_z, -1).wait_send()


def routed_by_lines(queries, span_keys, span_values, cache_keys, cache_values, routes, out_weight):
    blocks, heads = routes.shape[1:3]
    devices = lax.axis_size("ctx")
    stages = devices // 2
    rows = blocks * QB
    span = cache_keys.shape[0]
    columns = out_weight.shape[1] // lax.axis_size("head")
    named = jnp.any(
        routes[0][None] == jnp.arange(devices, dtype=jnp.int32)[:, None, None, None], axis=-1
    )
    flags = named.transpose(2, 1, 0).reshape(heads * blocks, devices).astype(jnp.bfloat16)
    flags = jnp.pad(flags, ((0, 0), (0, LANES - devices)))
    vmem = pl.BlockSpec(memory_space=pltpu.VMEM)
    anywhere = pl.BlockSpec(memory_space=pl.ANY)
    dma = pltpu.SemaphoreType.DMA
    return pl.pallas_call(
        functools.partial(kernel, stages, heads, blocks),
        out_shape=jax.ShapeDtypeStruct((rows, columns), jnp.bfloat16),
        in_specs=[anywhere, vmem] + [anywhere] * 5,
        out_specs=vmem,
        scratch_shapes=[
            pltpu.VMEM((stages, heads, rows, DH), jnp.bfloat16),
            pltpu.VMEM((heads, span, DH), jnp.bfloat16),
            pltpu.VMEM((heads, span, DH), jnp.bfloat16),
            pltpu.VMEM((stages, heads * blocks, LANES), jnp.bfloat16),
            pltpu.VMEM((stages, 2, heads * blocks, LANES), jnp.float32),
            pltpu.VMEM((heads, stages, DH, rows), jnp.bfloat16),
            pltpu.VMEM((heads, stages, 1, rows), jnp.float32),
            pltpu.VMEM((2, heads, stages, DH, rows), jnp.bfloat16),
            pltpu.VMEM((2, heads, stages, 1, rows), jnp.float32),
            pltpu.VMEM((heads, DH, rows), jnp.bfloat16),
            pltpu.VMEM((heads, 1, rows), jnp.float32),
            pltpu.VMEM((2, VALUE_ROWS, span), jnp.bfloat16),
            pltpu.VMEM((rows, 2 * heads * DH), jnp.bfloat16),
            pltpu.VMEM((2 * heads * DH, columns), jnp.bfloat16),
            pltpu.VMEM((rows, heads * DH), jnp.bfloat16),
            pltpu.VMEM((rows, heads * DH), jnp.bfloat16),
            pltpu.VMEM((span, heads * DH), jnp.bfloat16),
            pltpu.VMEM((span, heads * DH), jnp.bfloat16),
            dma((2, heads, stages)),
            dma((heads, stages)),
            dma((2, stages)),
            dma((stages,)),
            dma((heads, stages)),
            dma((2, heads, stages)),
            dma((heads, stages)),
            dma((2, heads, stages)),
            dma((2, heads)),
            dma((2, heads)),
            dma((heads,)),
            dma((heads,)),
            dma((3,)),
            dma((4,)),
            dma((heads,)),
        ],
        compiler_params=pltpu.CompilerParams(
            collective_id=0, has_side_effects=True, vmem_limit_bytes=60 * 2**20
        ),
        cost_estimate=pl.CostEstimate(
            flops=8 * stages * heads * rows * span * DH, bytes_accessed=2**24, transcendentals=0
        ),
    )(queries, flags, span_keys, span_values, cache_keys, cache_values, out_weight)


def on_device(queries, span_keys, span_values, cache_keys, cache_values, routes, out_weight):
    blocks, heads, top_picks = routes.shape[1:]
    devices = lax.axis_size("ctx")
    arguments = (queries, span_keys, span_values, cache_keys, cache_values, routes, out_weight)
    slots = max(2, 2 * blocks * heads * top_picks // devices)
    dense = slots >= blocks * heads and devices % 2 == 0 and devices <= LANES and lax.axis_size("head") == 2
    return (routed_by_lines if dense else routed_by_slots)(*arguments)


def solution(mesh):
    placed = (
        P(("groups", "ctx"), "head"),
        P(("groups", "ctx"), "head"),
        P(("groups", "ctx"), "head"),
        P(("groups", "ctx"), "head"),
        P(("groups", "ctx"), "head"),
        P("head", ("groups", "ctx"), None, None),
        P("head", None),
    )
    return jax.shard_map(
        on_device,
        mesh=mesh,
        in_specs=placed,
        out_specs=P(("groups", "ctx"), "head"),
        check_vma=False,
    )
```

```python
import functools
import math

import jax
import jax.numpy as jnp
from jax import lax
from jax.experimental import pallas as pl
from jax.experimental.pallas import tpu as pltpu
from jax.sharding import PartitionSpec as P

DH = 128
QB = 128


def shortened(value):

    def short(part):
        return part.astype(jnp.bfloat16) if part.dtype == jnp.float32 else part

    return jax.tree.map(short, value)


def soft_partial(scores, values_block, pattern):
    highest = jnp.max(scores, axis=-1, keepdims=True)
    exponent = jnp.exp(scores - highest)
    denominator = jnp.sum(exponent, axis=-1, keepdims=True)
    weights_low = (exponent / denominator).astype(jnp.bfloat16)
    result = jnp.einsum(
        pattern, weights_low, values_block, preferred_element_type=jnp.float32
    ).astype(jnp.bfloat16)
    log_total = highest[..., 0] + jnp.log(denominator[..., 0])
    return (result, log_total)


def routed_by_slots(queries, span_keys, span_values, cache_keys, cache_values, routes, out_weight):
    blocks = routes.shape[1]
    heads_here = routes.shape[2]
    top_picks = routes.shape[3]
    key_rows = cache_keys.shape[0]
    devices = lax.axis_size("ctx")
    scaling = 1.0 / math.sqrt(DH)
    blocked = queries.reshape(blocks, QB, heads_here, DH)
    most_rows = max(2, 2 * blocks * heads_here * top_picks // devices)
    groups = 1
    per_peer = groups * most_rows
    slot_total = per_peer * devices
    wanted = routes.reshape(-1)
    item_count = wanted.shape[0]
    item_ids = jnp.arange(item_count, dtype=jnp.int32)
    block_of = item_ids // (heads_here * top_picks)
    head_of = item_ids // top_picks % heads_here
    bucket = wanted * groups + block_of % groups
    one_hot = (bucket[:, None] == jnp.arange(devices * groups, dtype=jnp.int32)[None, :]).astype(
        jnp.int32
    )
    ranking = jnp.sum(jnp.cumsum(one_hot, axis=0) * one_hot, axis=1) - 1
    position = (block_of % groups * most_rows + ranking) * devices + wanted
    matches = position[None, :] == jnp.arange(slot_total, dtype=jnp.int32)[:, None]
    filled = jnp.any(matches, axis=1)
    source = jnp.sum(jnp.where(matches, item_ids[None, :], 0), axis=1)
    gathered = blocked[block_of[source], :, head_of[source], :]
    slot_queries = jnp.where(filled[:, None, None], gathered, jnp.zeros_like(gathered)).reshape(
        per_peer, devices, QB, DH
    )
    slot_heads = jnp.where(filled, head_of[source], 0).reshape(per_peer, devices)
    keys_by_head = cache_keys.reshape(key_rows, heads_here, DH).transpose(1, 0, 2)
    values_by_head = cache_values.reshape(key_rows, heads_here, DH).transpose(1, 0, 2)

    def one_portion(portion):
        queried, head_ids = portion
        chosen_keys = keys_by_head[head_ids]
        chosen_values = values_by_head[head_ids]
        scores = (
            jnp.einsum("pqd,pkd->pqk", queried, chosen_keys, preferred_element_type=jnp.float32)
            * scaling
        )
        return soft_partial(scores, chosen_values, "pqk,pkd->pqd")

    outputs, log_sums = lax.map(
        one_portion,
        (
            lax.all_to_all(slot_queries, "ctx", split_axis=1, concat_axis=1, tiled=True),
            lax.all_to_all(slot_heads, "ctx", split_axis=1, concat_axis=1, tiled=True),
        ),
    )
    outputs_back = jax.tree.map(
        lambda part, own: part.astype(own.dtype),
        lax.all_to_all(shortened(outputs), "ctx", split_axis=1, concat_axis=1, tiled=True),
        outputs,
    )
    sums_back = lax.all_to_all(log_sums, "ctx", split_axis=1, concat_axis=1, tiled=True)
    routed_out = outputs_back.reshape(slot_total, QB, DH)[position].reshape(
        blocks, heads_here, top_picks, QB, DH
    )
    routed_lse = sums_back.reshape(slot_total, QB)[position].reshape(
        blocks, heads_here, top_picks, QB
    )
    own_keys = span_keys.reshape(blocks, QB, heads_here, DH)
    own_values = span_values.reshape(blocks, QB, heads_here, DH)
    causal = jnp.arange(QB)[:, None] >= jnp.arange(QB)[None, :]
    self_scores = (
        jnp.einsum("bqhd,bkhd->bhqk", blocked, own_keys, preferred_element_type=jnp.float32)
        * scaling
    )
    self_scores = jnp.where(causal[None, None], self_scores, -jnp.inf)
    self_out, self_lse = soft_partial(self_scores, own_values, "bhqk,bkhd->bhqd")
    all_lse = jnp.concatenate([routed_lse, self_lse[:, :, None]], axis=2)
    all_out = jnp.concatenate(
        [routed_out.astype(jnp.float32), self_out[:, :, None].astype(jnp.float32)], axis=2
    )
    highest = jnp.max(all_lse, axis=2, keepdims=True)
    merge_weights = jnp.exp(all_lse - highest)
    merge_weights = merge_weights / jnp.sum(merge_weights, axis=2, keepdims=True)
    attention = jnp.sum(merge_weights[..., None] * all_out, axis=2)
    attention = (
        attention.transpose(0, 2, 1, 3).reshape(blocks * QB, heads_here * DH).astype(jnp.bfloat16)
    )
    partial_sums = jnp.dot(attention, out_weight, preferred_element_type=jnp.float32)
    return lax.psum_scatter(partial_sums, "head", scatter_dimension=1, tiled=True).astype(
        jnp.bfloat16
    )


BIG = 1e30
LOG2E = math.log2(math.e)
LANES = 128
HOP = 2
VALUE_ROWS = DH + 16


def store_partial(ref, lse_ref, out, lse):
    ref[...] = out.astype(jnp.bfloat16)
    lse_ref[...] = lse


def load_partial(ref, lse_ref):
    return ref[...].astype(jnp.float32), lse_ref[...]


def merged(first, second):
    out_a, lse_a = first
    out_b, lse_b = second
    top = jnp.maximum(lse_a, lse_b)
    weight_a = jnp.exp2(lse_a - top)
    weight_b = jnp.exp2(lse_b - top)
    total = weight_a + weight_b
    return (
        out_a * (weight_a / total) + out_b * (weight_b / total),
        top + jnp.log2(total),
    )


def kernel(
    stages,
    heads,
    blocks,
    q_hbm,
    flag_ref,
    span_k_hbm,
    span_v_hbm,
    k_hbm,
    v_hbm,
    w_hbm,
    y_ref,
    qg,
    kr,
    vr,
    fg,
    chosen_rows,
    part,
    part_lse,
    arrived,
    arrived_lse,
    selfp,
    self_lse,
    vt,
    att,
    wv,
    span_k,
    span_v,
    k_ref,
    v_ref,
    ag_send,
    ag_recv,
    flag_send,
    flag_recv,
    rs_send,
    rs_recv,
    lse_send,
    lse_recv,
    kv_send,
    kv_recv,
    att_send,
    att_recv,
    w_sem,
    own_sem,
    q_sem,
):
    rows = blocks * QB
    span = k_ref.shape[0]
    width = heads * DH
    columns = y_ref.shape[1]
    me = lax.axis_index("ctx")
    core = lax.axis_index("head")
    z = me // 2
    y = me % 2
    pair = me + 1 - 2 * y
    other = 1 - core
    last = stages - 1
    has_left = z > 0
    has_right = z < stages - 1
    scale = LOG2E / math.sqrt(DH)

    def head_columns(h):
        return pl.ds(pl.multiple_of(h * DH, DH), DH)

    barrier = pltpu.get_barrier_semaphore()
    pl.semaphore_signal(barrier, inc=1, device_id={"ctx": pair})
    pl.semaphore_signal(barrier, inc=1, device_id={"head": other})

    @pl.when(has_left)
    def _():
        pl.semaphore_signal(barrier, inc=1, device_id={"ctx": me - 2})

    @pl.when(has_right)
    def _():
        pl.semaphore_signal(barrier, inc=1, device_id={"ctx": me + 2})

    fg[z] = flag_ref[...]

    pl.semaphore_wait(
        barrier, 2 + jnp.minimum(z, 1) + jnp.minimum(stages - 1 - z, 1)
    )

    def kv_copies(h):
        return (
            pltpu.make_async_remote_copy(
                src_ref=k_hbm.at[:, head_columns(h)],
                dst_ref=kr.at[h],
                send_sem=kv_send.at[0, h],
                recv_sem=kv_recv.at[0, h],
                device_id={"ctx": pair},
            ),
            pltpu.make_async_remote_copy(
                src_ref=v_hbm.at[:, head_columns(h)],
                dst_ref=vr.at[h],
                send_sem=kv_send.at[1, h],
                recv_sem=kv_recv.at[1, h],
                device_id={"ctx": pair},
            ),
        )

    def q_copy(h):
        return pltpu.make_async_copy(q_hbm.at[:, head_columns(h)], qg.at[z, h], q_sem.at[h])

    own_copies = [
        pltpu.make_async_copy(source, target, own_sem.at[i])
        for i, (source, target) in enumerate(
            ((k_hbm, k_ref), (v_hbm, v_ref), (span_k_hbm, span_k), (span_v_hbm, span_v))
        )
    ]

    def ag_copy(h, source, step, own=False):
        return pltpu.make_async_remote_copy(
            src_ref=q_hbm.at[:, head_columns(h)] if own else qg.at[source, h],
            dst_ref=qg.at[source, h],
            send_sem=ag_send.at[(step + 1) // 2, h, source],
            recv_sem=ag_recv.at[h, source],
            device_id={"ctx": me + 2 * step},
        )

    def flag_copy(source, step):
        return pltpu.make_async_remote_copy(
            src_ref=fg.at[source],
            dst_ref=fg.at[source],
            send_sem=flag_send.at[(step + 1) // 2, source],
            recv_sem=flag_recv.at[source],
            device_id={"ctx": me + 2 * step},
        )

    def rs_copies(h, dest, step):
        side = (step + 1) // 2
        return (
            pltpu.make_async_remote_copy(
                src_ref=part.at[h, dest],
                dst_ref=arrived.at[side, h, dest],
                send_sem=rs_send.at[h, dest],
                recv_sem=rs_recv.at[side, h, dest],
                device_id={"ctx": me + 2 * step},
            ),
            pltpu.make_async_remote_copy(
                src_ref=part_lse.at[h, dest],
                dst_ref=arrived_lse.at[side, h, dest],
                send_sem=lse_send.at[h, dest],
                recv_sem=lse_recv.at[side, h, dest],
                device_id={"ctx": me + 2 * step},
            ),
        )

    def att_copy(h):
        place = pl.ds(pl.multiple_of(core * width + h * DH, DH), DH)
        return pltpu.make_async_remote_copy(
            src_ref=att.at[:, place],
            dst_ref=att.at[:, place],
            send_sem=att_send.at[h],
            recv_sem=att_recv.at[h],
            device_id={"head": other},
        )

    w_rows = pl.ds(pl.multiple_of(core * width, DH), width)
    w_remote = pltpu.make_async_remote_copy(
        src_ref=w_hbm.at[:, pl.ds(pl.multiple_of(other * columns, DH), columns)],
        dst_ref=wv.at[w_rows, :],
        send_sem=w_sem.at[0],
        recv_sem=w_sem.at[1],
        device_id={"head": other},
    )
    w_local = pltpu.make_async_copy(
        w_hbm.at[:, pl.ds(pl.multiple_of(core * columns, DH), columns)],
        wv.at[w_rows, :],
        w_sem.at[2],
    )

    def lead(step):
        return 2 * (last - z if step > 0 else z)

    def send_own(h, step):
        onward = has_right if step > 0 else has_left

        @pl.when((h < heads) & onward)
        def _():
            ag_copy(h, z, step, own=True).start()

        @pl.when((h == 0) & onward)
        def _():
            flag_copy(z, step).start()

    def gather_step(t):
        for step in (1, -1):
            send_own(t + lead(step), step)
        for a in range(1, stages):
            h = t - a

            @pl.when((h >= 0) & (h < heads))
            def _():
                for step in (1, -1):
                    source = z - a * step
                    here = (source >= 0) & (source < stages)
                    onward = has_right if step > 0 else has_left

                    @pl.when(here)
                    def _():
                        ag_copy(h, source, step).wait_recv()

                        @pl.when(onward)
                        def _():
                            ag_copy(h, source, step).start()

                        @pl.when(h == 0)
                        def _():
                            flag_copy(source, step).wait_recv()

                            @pl.when(onward)
                            def _():
                                flag_copy(source, step).start()

    def read_flags():
        for s in range(stages):
            flags = fg[s].astype(jnp.float32)
            lane = lax.broadcasted_iota(jnp.int32, flags.shape, 1)
            for at, number in enumerate((me, pair)):
                chosen = jnp.sum(
                    jnp.where(lane == number, flags, 0.0), axis=1, keepdims=True
                )
                chosen_rows[s, at] = jnp.broadcast_to(chosen, flags.shape)

    def prepare(h):
        for copy in kv_copies(h):
            copy.wait_recv()
        filler = jnp.ones((VALUE_ROWS - DH, span), jnp.bfloat16)
        for at, value in enumerate((v_ref[:, head_columns(h)], vr[h])):
            vt[at, 0:DH, :] = value.T
            vt[at, DH:VALUE_ROWS, :] = filler

    def compute(h, s):
        keys = (k_ref.at[:, head_columns(h)], kr.at[h])
        queried = qg[s, h]
        routed, scores, highest = [], [], None
        for at in range(2):
            chosen = jnp.concatenate(
                [chosen_rows[s, at, pl.ds(h * blocks + j, 1), :] for j in range(blocks)],
                axis=1,
            )
            score = lax.dot_general(
                keys[at][...],
                queried,
                (((1,), (1,)), ((), ())),
                preferred_element_type=jnp.float32,
            )
            top = jnp.where(
                chosen > 0.0, jnp.max(score, axis=0, keepdims=True) * scale, -BIG
            )
            highest = top if highest is None else jnp.maximum(highest, top)
            routed.append(chosen)
            scores.append(score)
        result = None
        for at in range(2):
            shift = jnp.where(routed[at] > 0.0, highest, BIG)
            exponent = jnp.exp2(scores[at] * scale - shift).astype(jnp.bfloat16)
            product = jnp.dot(vt[at], exponent, preferred_element_type=jnp.float32)
            result = product if result is None else result + product
        total = result[DH : DH + 1, :]
        safe = jnp.maximum(total, 0.5)
        store_partial(
            part.at[h, s],
            part_lse.at[h, s],
            result[0:DH, :] * (1.0 / safe),
            jnp.where(total > 0.0, highest + jnp.log2(safe), -BIG),
        )

    def self_part(h):
        for j in range(blocks):
            here = pl.ds(j * QB, QB)
            score = lax.dot_general(
                span_k[here, head_columns(h)],
                qg[z, h, here, :],
                (((1,), (1,)), ((), ())),
                preferred_element_type=jnp.float32,
            )
            shape = (QB, QB)
            causal = lax.broadcasted_iota(jnp.int32, shape, 0) <= lax.broadcasted_iota(
                jnp.int32, shape, 1
            )
            score = jnp.where(causal, score * scale, -BIG)
            top = jnp.max(score, axis=0, keepdims=True)
            exponent = jnp.exp2(score - top)
            total = jnp.sum(exponent, axis=0, keepdims=True)
            out = jnp.dot(
                span_v[here, head_columns(h)].T,
                exponent.astype(jnp.bfloat16),
                preferred_element_type=jnp.float32,
            )
            store_partial(
                selfp.at[h, :, j * QB : (j + 1) * QB],
                self_lse.at[h, :, j * QB : (j + 1) * QB],
                out * (1.0 / total),
                top + jnp.log2(total),
            )

    def at_end(step):
        return ~has_left if step > 0 else ~has_right

    def reduce_step(h, step):
        side = (step + 1) // 2

        @pl.when((h >= 0) & (h < heads) & ~at_end(step))
        def _():
            for dest in reversed(range(stages)) if step > 0 else range(stages):
                ahead = (dest - z) * step

                @pl.when(ahead >= 0)
                def _():
                    for copy in rs_copies(h, dest, step):
                        copy.wait_recv()
                    mine = (part.at[h, dest], part_lse.at[h, dest])
                    store_partial(
                        *mine,
                        *merged(
                            load_partial(*mine),
                            load_partial(
                                arrived.at[side, h, dest], arrived_lse.at[side, h, dest]
                            ),
                        ),
                    )

                @pl.when(ahead > 0)
                def _():
                    for copy in rs_copies(h, dest, step):
                        copy.start()

    def finish(h):
        out, _ = merged(
            load_partial(part.at[h, z], part_lse.at[h, z]),
            load_partial(selfp.at[h], self_lse.at[h]),
        )
        place = pl.ds(pl.multiple_of(core * width + h * DH, DH), DH)
        att[:, place] = out.T.astype(jnp.bfloat16)
        att_copy(h).start()

    for step in (1, -1):

        @pl.loop(0, lead(step) + 1)
        def _(h):
            send_own(h, step)

    @pl.loop(0, heads)
    def _(h):
        for copy in kv_copies(h):
            copy.start()

    w_remote.start()
    w_local.start()

    @pl.loop(0, heads)
    def _(h):
        q_copy(h).start()

    for copy in own_copies:
        copy.start()

    @pl.loop(0, heads)
    def _(h):
        q_copy(h).wait()

    @pl.loop(1, heads + last + HOP * last + 1)
    def _(t):
        gather_step(t)
        h = t - last
        busy = (h >= 0) & (h < heads)

        @pl.when(h == 0)
        def _():
            read_flags()
            for copy in own_copies:
                copy.wait()

        reduce_step(h - HOP * z, 1)
        reduce_step(h - HOP * (last - z), -1)

        @pl.when(busy)
        def _():
            prepare(h)
            for i in range(stages):
                s = jnp.where(2 * z >= stages, i, last - i)
                compute(h, s)
                for step in (1, -1):

                    @pl.when(((s - z) * step > 0) & at_end(step))
                    def _():
                        for copy in rs_copies(h, s, step):
                            copy.start()

        @pl.when(busy)
        def _():
            self_part(h)

        done = h - HOP * last

        @pl.when((done >= 0) & (done < heads))
        def _():
            finish(done)

    w_local.wait()
    w_remote.wait()

    @pl.loop(0, heads)
    def _(h):
        att_copy(h).wait_recv()

    tile = math.gcd(columns, 512)

    @pl.loop(0, columns // tile)
    def _(n):
        here = pl.ds(pl.multiple_of(n * tile, tile), tile)
        y_ref[:, here] = jnp.dot(
            att[...], wv[:, here], preferred_element_type=jnp.float32
        ).astype(jnp.bfloat16)

    @pl.loop(0, heads)
    def _(h):
        att_copy(h).wait_send()
        for copy in kv_copies(h):
            copy.wait_send()
        for other_z in range(stages):

            @pl.when((other_z <= z) & has_right)
            def _():
                ag_copy(h, other_z, 1).wait_send()

            @pl.when((other_z >= z) & has_left)
            def _():
                ag_copy(h, other_z, -1).wait_send()

            for step in (1, -1):

                @pl.when((other_z - z) * step > 0)
                def _():
                    for copy in rs_copies(h, other_z, step):
                        copy.wait_send()

    for other_z in range(stages):

        @pl.when((other_z <= z) & has_right)
        def _():
            flag_copy(other_z, 1).wait_send()

        @pl.when((other_z >= z) & has_left)
        def _():
            flag_copy(other_z, -1).wait_send()


def routed_by_lines(queries, span_keys, span_values, cache_keys, cache_values, routes, out_weight):
    blocks, heads = routes.shape[1:3]
    devices = lax.axis_size("ctx")
    stages = devices // 2
    rows = blocks * QB
    span = cache_keys.shape[0]
    columns = out_weight.shape[1] // lax.axis_size("head")
    named = jnp.any(
        routes[0][None] == jnp.arange(devices, dtype=jnp.int32)[:, None, None, None], axis=-1
    )
    flags = named.transpose(2, 1, 0).reshape(heads * blocks, devices).astype(jnp.bfloat16)
    flags = jnp.pad(flags, ((0, 0), (0, LANES - devices)))
    vmem = pl.BlockSpec(memory_space=pltpu.VMEM)
    anywhere = pl.BlockSpec(memory_space=pl.ANY)
    dma = pltpu.SemaphoreType.DMA
    return pl.pallas_call(
        functools.partial(kernel, stages, heads, blocks),
        out_shape=jax.ShapeDtypeStruct((rows, columns), jnp.bfloat16),
        in_specs=[anywhere, vmem] + [anywhere] * 5,
        out_specs=vmem,
        scratch_shapes=[
            pltpu.VMEM((stages, heads, rows, DH), jnp.bfloat16),
            pltpu.VMEM((heads, span, DH), jnp.bfloat16),
            pltpu.VMEM((heads, span, DH), jnp.bfloat16),
            pltpu.VMEM((stages, heads * blocks, LANES), jnp.bfloat16),
            pltpu.VMEM((stages, 2, heads * blocks, LANES), jnp.float32),
            pltpu.VMEM((heads, stages, DH, rows), jnp.bfloat16),
            pltpu.VMEM((heads, stages, 1, rows), jnp.float32),
            pltpu.VMEM((2, heads, stages, DH, rows), jnp.bfloat16),
            pltpu.VMEM((2, heads, stages, 1, rows), jnp.float32),
            pltpu.VMEM((heads, DH, rows), jnp.bfloat16),
            pltpu.VMEM((heads, 1, rows), jnp.float32),
            pltpu.VMEM((2, VALUE_ROWS, span), jnp.bfloat16),
            pltpu.VMEM((rows, 2 * heads * DH), jnp.bfloat16),
            pltpu.VMEM((2 * heads * DH, columns), jnp.bfloat16),
            pltpu.VMEM((rows, heads * DH), jnp.bfloat16),
            pltpu.VMEM((rows, heads * DH), jnp.bfloat16),
            pltpu.VMEM((span, heads * DH), jnp.bfloat16),
            pltpu.VMEM((span, heads * DH), jnp.bfloat16),
            dma((2, heads, stages)),
            dma((heads, stages)),
            dma((2, stages)),
            dma((stages,)),
            dma((heads, stages)),
            dma((2, heads, stages)),
            dma((heads, stages)),
            dma((2, heads, stages)),
            dma((2, heads)),
            dma((2, heads)),
            dma((heads,)),
            dma((heads,)),
            dma((3,)),
            dma((4,)),
            dma((heads,)),
        ],
        compiler_params=pltpu.CompilerParams(
            collective_id=0, has_side_effects=True, vmem_limit_bytes=60 * 2**20
        ),
        cost_estimate=pl.CostEstimate(
            flops=8 * stages * heads * rows * span * DH, bytes_accessed=2**24, transcendentals=0
        ),
    )(queries, flags, span_keys, span_values, cache_keys, cache_values, out_weight)


def on_device(queries, span_keys, span_values, cache_keys, cache_values, routes, out_weight):
    blocks, heads, top_picks = routes.shape[1:]
    devices = lax.axis_size("ctx")
    arguments = (queries, span_keys, span_values, cache_keys, cache_values, routes, out_weight)
    slots = max(2, 2 * blocks * heads * top_picks // devices)
    dense = slots >= blocks * heads and devices % 2 == 0 and devices <= LANES and lax.axis_size("head") == 2
    return (routed_by_lines if dense else routed_by_slots)(*arguments)


def solution(mesh):
    placed = (
        P(("groups", "ctx"), "head"),
        P(("groups", "ctx"), "head"),
        P(("groups", "ctx"), "head"),
        P(("groups", "ctx"), "head"),
        P(("groups", "ctx"), "head"),
        P("head", ("groups", "ctx"), None, None),
        P("head", None),
    )
    return jax.shard_map(
        on_device,
        mesh=mesh,
        in_specs=placed,
        out_specs=P(("groups", "ctx"), "head"),
        check_vma=False,
    )
```
